32 devices in a mesh: dp: 8 (over y, x, core), tensor: 4 (over z).
Axes of the slice: x: 2, y: 2, z: 4, core: 2. Of those that a mesh axis runs over, the one named last changes fastest.
Arguments:
- short_tokens: bfloat16 [16, 256, 768], P('dp'), may hold values from -6 to 6
- short_lengths: int32 [16], P('dp'), may hold values from 64 to 256, as said below
- long_tokens: bfloat16 [24, 512, 768], P('dp'), may hold values from -6 to 6
- long_lengths: int32 [24], P('dp'), may hold values from 257 to 512, as said below
- w_qkv: bfloat16 [3, 768, 768], P(None, None, 'tensor'), may hold values from -0.21875 to 0.21875
- b_qv: bfloat16 [2, 12, 64], P(None, 'tensor'), may hold values from -3 to 3
- w_out: bfloat16 [768, 768], P('tensor'), may hold values from -2.5 to 2.5
- res_biases: bfloat16 [2, 768], replicated, may hold values from -3 to 3
- ln_gains: bfloat16 [2, 768], replicated, may hold values from 0.099609375 to 1.8984375
- ln_shifts: bfloat16 [2, 768], replicated, may hold values from -3 to 3
- w_up: bfloat16 [768, 3072], P(None, 'tensor'), may hold values from -0.21875 to 0.21875
- b_up: bfloat16 [4, 768], P('tensor'), may hold values from -3 to 3
- w_down: bfloat16 [3072, 768], P('tensor'), may hold values from -0.109375 to 0.109375
- short_cotangent: bfloat16 [16, 256, 768], P('dp'), may hold values from -6 to 6
- long_cotangent: bfloat16 [24, 512, 768], P('dp'), may hold values from -6 to 6
Outputs:
- short_encoded: bfloat16 [16, 256, 768], P('dp')
- long_encoded: bfloat16 [24, 512, 768], P('dp')
- short_grad_tokens: float32 [16, 256, 768], P('dp')
- long_grad_tokens: float32 [24, 512, 768], P('dp')
- grad_qkv: float32 [3, 768, 768], P(None, 'dp', 'tensor')
- grad_qv_bias: float32 [2, 12, 64], P(None, 'tensor', 'dp')
- grad_out: float32 [768, 768], P('tensor', 'dp')
- grad_res_biases: float32 [2, 768], P(None, 'dp')
- grad_gains: float32 [2, 768], P(None, 'dp')
- grad_shifts: float32 [2, 768], P(None, 'dp')
- grad_up: float32 [768, 3072], P('dp', 'tensor')
- grad_up_bias: float32 [4, 768], P('tensor', 'dp')
- grad_down: float32 [3072, 768], P('tensor', 'dp')
The draws below stay inside these ranges and needn't reach their ends.
Inputs may be any that keep to these rules, and one draw needn't show every extreme that they name: `short_lengths`: the first short pair has 256 valid tokens. `long_lengths`: the first long pair has 512 valid tokens.
All inputs are finite; a program needn't handle non-finite values.
Results may differ from the reference program's by a relative error of at most 0.013.
The reference program's roundings to bfloat16 on the way count: a program that leaves them out, or rounds other values in their place, can miss the bound.
Values sent between devices are 32-bit elements; how exact they have to be, the bound alone decides.
No kernel may reach another device: no remote copies, remote signals or barrier semaphores. Data moves between devices by JAX's collectives and lax.ppermute only.
A program may use at most 128 MiB of HBM per device.

```python
import jax
import jax.numpy as jnp
from jax import lax

D = 768
HEADS = 12
HD = 64
FF = 3072
SLOT = 512
SHORT_SLOT = 256
SHORT_PAIRS = 16
LONG_PAIRS = 24
FF_DEV = 768
N_TENSOR = 4


def draw_short_lengths(key, part):
    chosen = jax.random.randint(key, (SHORT_PAIRS,), SLOT // 8, SLOT // 2 + 1)
    chosen = chosen.at[0].set(SLOT // 2)
    return chosen.astype(jnp.int32)


def draw_long_lengths(key, part):
    chosen = jax.random.randint(jax.random.fold_in(key, 7), (LONG_PAIRS,), SLOT // 2 + 1, SLOT + 1)
    chosen = chosen.at[0].set(SLOT)
    return chosen.astype(jnp.int32)


def spiked(values, key, source, target, blocks, factor):
    owner, partner = [(jnp.arange(values.shape[position]) // (values.shape[position] // blocks)).reshape([-1 if axis == position else 1 for axis in range(values.ndim)]) for position in (source, target)]
    chosen = jax.random.permutation(key, blocks)[partner]
    strong = (owner == chosen) | (owner == (partner + blocks // 2) % blocks)
    return jnp.where(strong, factor * values, values)


def steps_of(own_key, extent, cuts, least, high):
    factor_of, own = 1.0, jax.random.fold_in(own_key, 6)
    for position, blocks in cuts:
        draws = jnp.exp(jax.random.uniform(jax.random.fold_in(own, position), (blocks,), jnp.float32, least / len(cuts), high / len(cuts)))
        factor_of = factor_of * jnp.repeat(draws, extent[position] // blocks).reshape([-1 if axis == position else 1 for axis in range(len(extent))])
    return factor_of


def gaussian(key, dims, width, reach, shards=(), dtype=jnp.bfloat16):
    array = jax.random.normal(key, dims, jnp.float32) * width
    if len(shards) > 0:
        array = steps_of(key, dims, shards, -0.22, 0.18) * array
    return jnp.clip(array, min=-reach, max=reach).astype(dtype)


def gaussian_with(rng, extent, scale, reach, pieces, heavy, held_as=jnp.bfloat16):
    entries = scale * jax.random.normal(rng, extent, jnp.float32)
    if pieces:
        entries = entries * steps_of(rng, extent, pieces, -0.22, 0.18)
    return jnp.clip(spiked(entries, jax.random.fold_in(rng, 3), *heavy), -reach, reach).astype(held_as)


def setup_inputs(seed: int = 0) -> dict:
    keys = jax.random.split(jax.random.key(seed), 16)
    return {
        "short_tokens": gaussian_with(keys[0], (SHORT_PAIRS, SHORT_SLOT, D), 1.0, 6.0, ((0, 8),), (0, 2, 8, 2.0)),
        "short_lengths": draw_short_lengths(jax.random.fold_in(keys[15], 71), 0),
        "long_tokens": gaussian_with(keys[2], (LONG_PAIRS, SLOT, D), 1.0, 6.0, ((0, 8),), (0, 2, 8, 2.0)),
        "long_lengths": draw_long_lengths(jax.random.fold_in(keys[15], 71), 0),
        "w_qkv": gaussian(keys[4], (3, D, D), D ** -0.5, 0.21875, ((2, 4),)),
        "b_qv": gaussian(keys[5], (2, HEADS, HD), 0.5, 3.0, ((1, 4),)),
        "w_out": gaussian(keys[6], (D, D), (D // 128) ** -0.5, 2.5, ((0, 4),)),
        "res_biases": gaussian(keys[7], (2, D), 0.5, 3.0),
        "ln_gains": jnp.clip(1.0 + 0.18 * jax.random.normal(keys[8], (2, D), jnp.float32), 0.099609375, 1.8984375).astype(jnp.bfloat16),
        "ln_shifts": gaussian(keys[9], (2, D), 0.5, 3.0),
        "w_up": gaussian(keys[10], (D, FF), D ** -0.5, 0.21875, ((1, 4),)),
        "b_up": gaussian(keys[11], (N_TENSOR, FF_DEV), 0.5, 3.0, ((0, 4),)),
        "w_down": gaussian(keys[12], (FF, D), FF ** -0.5, 0.109375, ((0, 4),)),
        "short_cotangent": gaussian_with(keys[13], (SHORT_PAIRS, SHORT_SLOT, D), 1.0, 6.0, ((0, 8),), (0, 2, 8, 2.0)),
        "long_cotangent": gaussian_with(keys[14], (LONG_PAIRS, SLOT, D), 1.0, 6.0, ((0, 8),), (0, 2, 8, 2.0)),
    }


HIGHEST_PRECISION = lax.Precision.HIGHEST
EPSILON = 1e-12

@jax.custom_vjp
def low(v):
    return lax.optimization_barrier(v.astype(jnp.bfloat16)).astype(jnp.float32)

@jax.custom_vjp
def low_back(v):
    return v

def low_keep(v):
    return (low(v), None)

def low_pass(kept, grad):
    return (grad,)

def back_keep(v):
    return (v, None)

def back_low(kept, grad):
    return (low(grad),)
low.defvjp(low_keep, low_pass)
low_back.defvjp(back_keep, back_low)

def normalize(hidden, gain, shift):
    center = hidden - lax.optimization_barrier(jnp.mean(hidden, -1, keepdims=True))
    factor = lax.rsqrt(lax.optimization_barrier(jnp.mean(center * center, -1, keepdims=True)) + EPSILON)
    return center * factor * gain + shift

def attend_pair(inputs):
    queries, key_rows, value_rows, length = inputs
    scores = jnp.einsum('qhe,khe->hqk', queries, key_rows, precision=HIGHEST_PRECISION) * HD ** (-0.5)
    scores = low_back(scores)
    visible = jnp.arange(key_rows.shape[0]) < length
    scores = jnp.where(visible[None, None, :], scores, -1e+30)
    largest = lax.optimization_barrier(jnp.max(scores, -1, keepdims=True))
    weights_exp = jnp.exp(scores - largest)
    probs = weights_exp / lax.optimization_barrier(jnp.sum(weights_exp, -1, keepdims=True))
    return jnp.einsum('hqk,khe->qhe', low(probs), value_rows, precision=HIGHEST_PRECISION)

def layer(params, tokens_group, lengths_group):
    w_qkv, b_qv, w_out, res_biases, ln_gains, ln_shifts, w_up, b_up, w_down = params
    slot_len = tokens_group.shape[1]
    flat = tokens_group.reshape(-1, D)
    projected = jnp.einsum('rd,cde->cre', flat, w_qkv, precision=HIGHEST_PRECISION)
    bias_rows = jnp.stack([b_qv[0].reshape(D), jnp.zeros((D,), jnp.float32), b_qv[1].reshape(D)])
    projected = low(low_back(projected + bias_rows[:, None, :]))
    split = projected.reshape(3, -1, slot_len, HEADS, HD)
    mixed = lax.map(jax.checkpoint(attend_pair), (split[0], split[1], split[2], lengths_group))
    mixed = low(low_back(mixed.reshape(-1, D)))
    attn_sum = low_back(jnp.dot(mixed, w_out, precision=HIGHEST_PRECISION))
    normed_one = normalize(flat + attn_sum + res_biases[0], ln_gains[0], ln_shifts[0])
    inner = low_back(jnp.dot(low(normed_one), w_up, precision=HIGHEST_PRECISION) + b_up.reshape(FF))
    activated = low(jax.nn.gelu(inner, approximate=False))
    ffn_sum = low_back(jnp.dot(activated, w_down, precision=HIGHEST_PRECISION))
    result = normalize(normed_one + ffn_sum + res_biases[1], ln_gains[1], ln_shifts[1])
    return result.reshape(tokens_group.shape)

def bucket_pass(params, totals, tokens, lengths, cotangent):
    pair_count, slot_len = (tokens.shape[0], tokens.shape[1])
    group_count = pair_count // 8
    token_groups = tokens.astype(jnp.float32).reshape(group_count, 8, slot_len, D)
    length_groups = lengths.reshape(group_count, 8)
    cot_groups = cotangent.astype(jnp.float32).reshape(group_count, 8, slot_len, D)

    def one_group(running, group_item):
        group_tokens, group_lengths, group_cot = group_item
        result, pullback = jax.vjp(lambda weights, inputs: layer(weights, inputs, group_lengths), params, group_tokens)
        grads, grad_input = pullback(group_cot)
        return (jax.tree.map(jnp.add, running, grads), (result.astype(jnp.bfloat16), grad_input))
    running, (encoded, grad_input) = lax.scan(one_group, totals, (token_groups, length_groups, cot_groups))
    return (running, encoded.reshape(pair_count, slot_len, D), grad_input.reshape(pair_count, slot_len, D))

def reference(short_tokens, short_lengths, long_tokens, long_lengths, w_qkv, b_qv, w_out, res_biases, ln_gains, ln_shifts, w_up, b_up, w_down, short_cotangent, long_cotangent):
    params = jax.tree.map(lambda operand: operand.astype(jnp.float32), (w_qkv, b_qv, w_out, res_biases, ln_gains, ln_shifts, w_up, b_up, w_down))
    zero_grads = jax.tree.map(jnp.zeros_like, params)
    totals, short_encoded, short_grad = bucket_pass(params, zero_grads, short_tokens, short_lengths, short_cotangent)
    totals, long_encoded, long_grad = bucket_pass(params, totals, long_tokens, long_lengths, long_cotangent)
    g_qkv, g_bqv, g_out, g_res, g_gains, g_shifts, g_up, g_bup, g_down = totals
    return (short_encoded, long_encoded, short_grad, long_grad, g_qkv, g_bqv, g_out, g_res, g_gains, g_shifts, g_up, g_bup, g_down)
```

```python
import jax
import jax.numpy as jnp
import numpy as np
from jax import lax
from jax.experimental import pallas as pl
from jax.experimental.pallas import tpu as pltpu
from jax.sharding import PartitionSpec as P

HD = 64
EPS = 1e-12
BF = jnp.bfloat16
F32 = jnp.float32
NT = (((1,), (1,)), ((), ()))
TN = (((0,), (0,)), ((), ()))


def dot(a, b, dims=(((1,), (0,)), ((), ()))):
    return lax.dot_general(a, b, dims, preferred_element_type=F32)


def lanes(width, test):
    lane = lax.broadcasted_iota(jnp.int32, (1, width), 1)
    return jnp.where(test(lane), 1.0, 0.0).astype(F32)


def head_row(h, width, extra):
    w = width * HD

    def test(lane):
        own = (lane >= h * HD) & (lane < (h + 1) * HD)
        if extra:
            own = own | ((lane >= w + 1 + 3 * h) & (lane < w + 4 + 3 * h))
        return own

    return test


def split3(x):
    hi = x.astype(BF).astype(F32)
    rest = x - hi
    mid = rest.astype(BF).astype(F32)
    return hi, mid, rest - mid


def attn_fwd_kernel(
    sp_ref, len_ref, x_ref, w_ref, b_ref, *refs, nshort, short_slot, heads, blk
):
    p_ref, o_ref, w_s = refs[-3:]
    hw = heads * HD
    g, b = pl.program_id(0), pl.program_id(1)
    sub = blk // short_slot
    long0 = nshort // sub

    @pl.when(b == 0)
    def _():
        w_s[...] = jnp.zeros_like(w_s)
        for c in range(3):
            w_s[256 * c : 256 * c + hw] = w_ref[0, c * hw : (c + 1) * hw].astype(BF)

    p_ref[0] = (dot(x_ref[...], w_s[...], NT) + b_ref[0]).astype(BF)

    def pair(row, rows, length):
        sl = pl.ds(row, rows)
        pos = lax.broadcasted_iota(jnp.int32, (rows, 1), 0)
        hidden = jnp.where(pos < length, 0.0, -1e30)
        at_mask = lanes(256, lambda l: l == hw)
        q = (p_ref[0, sl, 0:256].astype(F32) * 0.125 + at_mask).astype(BF)
        k = (p_ref[0, sl, 256:512].astype(F32) + hidden * at_mask).astype(BF)
        v = p_ref[0, sl, 512:768]
        p_ref[0, sl, 256:512] = k
        out = jnp.zeros((rows, 256), F32)
        ext = jnp.zeros((rows, 256), F32)
        for h in range(heads):
            own = lanes(256, head_row(h, heads, False))
            s = dot(q * (own + at_mask).astype(BF), k, NT)
            m = jnp.max(s, axis=1, keepdims=True)
            e = jnp.exp(s - m)
            total = jnp.sum(e, axis=1, keepdims=True)
            a = (e * (1.0 / total)).astype(BF)
            out = out + dot(a, v * own.astype(BF))
            for i, part in enumerate(split3(-(m + jnp.log(total)))):
                ext = ext + part * lanes(256, lambda l: l == hw + 1 + 3 * h + i)
        p_ref[0, sl, 0:256] = (q.astype(F32) + ext).astype(BF)
        o_ref[0, sl] = out.astype(BF)

    @pl.when(b < long0)
    def _():
        for i in range(sub):
            pair(i * short_slot, short_slot, len_ref[b * sub + i])

    @pl.when(b >= long0)
    def _():
        pair(0, blk, len_ref[nshort + b - long0])


def attn_fwd(groups, lens, x, w, bias, prev, nshort, short_slot, heads, blk, w_index):
    rows, d = x.shape
    nb = rows // blk
    tensor = bias.shape[0]
    n = groups.shape[0]
    wrows = 3 * heads * HD

    def out_map(g, b, sp, ln):
        return (sp[g], b, 0)

    in_specs = [
        pl.BlockSpec((blk, d), lambda g, b, sp, ln: (b, 0)),
        pl.BlockSpec((1, wrows, d), lambda g, b, sp, ln: (w_index(g, sp), 0, 0)),
        pl.BlockSpec((1, 1, 768), lambda g, b, sp, ln: (sp[g], 0, 0)),
    ]
    args = [x, w, bias]
    aliases = {}
    if prev is not None:
        in_specs += [pl.BlockSpec(memory_space=pl.ANY)] * 2
        args += list(prev)
        aliases = {5: 0, 6: 1}
    return pl.pallas_call(
        lambda *r: attn_fwd_kernel(
            *r, nshort=nshort, short_slot=short_slot, heads=heads, blk=blk
        ),
        grid_spec=pltpu.PrefetchScalarGridSpec(
            num_scalar_prefetch=2,
            grid=(n, nb),
            in_specs=in_specs,
            out_specs=[
                pl.BlockSpec((1, blk, 768), out_map),
                pl.BlockSpec((1, blk, 256), out_map),
            ],
            scratch_shapes=[pltpu.VMEM((768, d), BF)],
        ),
        out_shape=[
            jax.ShapeDtypeStruct((tensor, rows, 768), BF),
            jax.ShapeDtypeStruct((tensor, rows, 256), BF),
        ],
        input_output_aliases=aliases,
        compiler_params=pltpu.CompilerParams(vmem_limit_bytes=60 * 2**20),
        name="attn_fwd",
    )(groups, lens, *args)


def attn_bwd_pair(refs, sl, rows, heads):
    p_ref, o_ref, do_ref = refs
    hw = heads * HD
    q, k, v = p_ref[0, sl, 0:256], p_ref[0, sl, 256:512], p_ref[0, sl, 512:768]
    do = do_ref[0, sl]
    do32 = do.astype(F32)
    prod = do32 * o_ref[0, sl].astype(F32)
    ext = do32
    for h in range(heads):
        own = lanes(256, head_row(h, heads, False))
        delta = jnp.sum(prod * own, axis=1, keepdims=True)
        for i, part in enumerate(split3(-delta)):
            ext = ext + part * lanes(256, lambda l: l == hw + 1 + 3 * h + i)
    do_ext = ext.astype(BF)
    kt = k.T
    at_mask = lanes(256, lambda l: l == hw)
    dk = jnp.zeros((rows, 256), F32)
    dv = jnp.zeros((rows, 256), F32)
    dqs = []
    for h in range(heads):
        row = lanes(256, head_row(h, heads, True))
        qh = q * (row + at_mask).astype(BF)
        doh = do_ext * row.astype(BF)
        p = jnp.exp(dot(k, qh, NT))
        ds = (p * dot(v, doh, NT)).astype(BF)
        dv = dv + dot(p.astype(BF), doh)
        dk = dk + dot(ds, qh)
        dqs.append(dot(kt[h * HD : (h + 1) * HD], ds))
    dqs.append(jnp.zeros((256 - hw, rows), F32))
    dq = jnp.concatenate(dqs, 0).T * 0.125
    real = lanes(256, lambda l: l < hw)
    return dq.astype(BF), (dk * real).astype(BF), (dv * real).astype(BF)


def over_pairs(b, refs, dst, *, nshort, short_slot, heads, blk):
    sub = blk // short_slot
    long0 = nshort // sub

    def one(row, rows):
        sl = pl.ds(row, rows)
        for c, val in enumerate(attn_bwd_pair(refs, sl, rows, heads)):
            dst(sl, c, val)

    @pl.when(b < long0)
    def _():
        for i in range(sub):
            one(i * short_slot, short_slot)

    @pl.when(b >= long0)
    def _():
        one(0, blk)


def bwd_own_kernel(sp_ref, x_ref, p_ref, o_ref, do_ref, dp_ref, gw_ref, gb_ref, **kw):
    b = pl.program_id(0)

    def dst(sl, c, val):
        dp_ref[sl, 256 * c : 256 * (c + 1)] = val

    over_pairs(b, (p_ref, o_ref, do_ref), dst, **kw)
    dp = dp_ref[...]
    gw = dot(x_ref[...], dp, TN)
    gb = jnp.sum(dp.astype(F32).reshape(-1, 8, 768), axis=0)

    @pl.when(b == 0)
    def _():
        gw_ref[...] = gw
        gb_ref[...] = gb

    @pl.when(b > 0)
    def _():
        gw_ref[...] += gw
        gb_ref[...] += gb


def bwd_own(own, x, p, o, do, blk, **kw):
    rows, d = x.shape
    return pl.pallas_call(
        lambda *r: bwd_own_kernel(*r, blk=blk, **kw),
        grid_spec=pltpu.PrefetchScalarGridSpec(
            num_scalar_prefetch=1,
            grid=(rows // blk,),
            in_specs=[
                pl.BlockSpec((blk, d), lambda b, sp: (b, 0)),
                pl.BlockSpec((1, blk, 768), lambda b, sp: (sp[0], b, 0)),
                pl.BlockSpec((1, blk, 256), lambda b, sp: (sp[0], b, 0)),
                pl.BlockSpec((1, blk, 256), lambda b, sp: (sp[0], b, 0)),
            ],
            out_specs=[
                pl.BlockSpec((blk, 768), lambda b, sp: (b, 0)),
                pl.BlockSpec((d, 768), lambda b, sp: (0, 0)),
                pl.BlockSpec((8, 768), lambda b, sp: (0, 0)),
            ],
        ),
        out_shape=[
            jax.ShapeDtypeStruct((rows, 768), BF),
            jax.ShapeDtypeStruct((d, 768), F32),
            jax.ShapeDtypeStruct((8, 768), F32),
        ],
        compiler_params=pltpu.CompilerParams(vmem_limit_bytes=60 * 2**20),
        name="attn_bwd_own",
    )(own, x, p, o, do)


def bwd_rest_kernel(sp_ref, p_ref, o_ref, do_ref, own_ref, dh_ref, w_ref, gx_ref, dp_s, w_s, **kw):
    b, g = pl.program_id(0), pl.program_id(1)
    tensor = w_s.shape[0]
    hw = kw["heads"] * HD
    me = sp_ref[0]
    grp = sp_ref[1 + g]

    @pl.when((b == 0) & (g == 0))
    def _():
        w_s[...] = jnp.zeros_like(w_s)
        for j in range(tensor):
            for c in range(3):
                w_s[j, 256 * c : 256 * c + hw] = w_ref[j, c * hw : (c + 1) * hw].astype(BF)

    @pl.when(g == 0)
    def _():
        dp_s[me] = own_ref[...]

    def dst(sl, c, val):
        dp_s[grp, sl, 256 * c : 256 * (c + 1)] = val

    over_pairs(b, (p_ref, o_ref, do_ref), dst, **kw)

    @pl.when(g == tensor - 2)
    def _():
        acc = dh_ref[...]
        for j in range(tensor):
            acc = acc + dot(dp_s[j], w_s[j])
        gx_ref[...] = acc


def bwd_rest(sp, p, o, do, own_dp, dh, w, blk, **kw):
    tensor, rows, _ = p.shape
    d = dh.shape[1]
    wrows = 3 * kw["heads"] * HD

    def grp_map(b, g, sp):
        return (sp[1 + g], b, 0)

    return pl.pallas_call(
        lambda *r: bwd_rest_kernel(*r, blk=blk, **kw),
        grid_spec=pltpu.PrefetchScalarGridSpec(
            num_scalar_prefetch=1,
            grid=(rows // blk, tensor - 1),
            in_specs=[
                pl.BlockSpec((1, blk, 768), grp_map),
                pl.BlockSpec((1, blk, 256), grp_map),
                pl.BlockSpec((1, blk, 256), grp_map),
                pl.BlockSpec((blk, 768), lambda b, g, sp: (b, 0)),
                pl.BlockSpec((blk, d), lambda b, g, sp: (b, 0)),
                pl.BlockSpec((tensor, wrows, d), lambda b, g, sp: (0, 0, 0), pipeline_mode=pl.Buffered(1)),
            ],
            out_specs=pl.BlockSpec((blk, d), lambda b, g, sp: (b, 0)),
            scratch_shapes=[
                pltpu.VMEM((tensor, blk, 768), BF),
                pltpu.VMEM((tensor, 768, d), BF),
            ],
        ),
        out_shape=jax.ShapeDtypeStruct((rows, d), F32),
        compiler_params=pltpu.CompilerParams(vmem_limit_bytes=60 * 2**20),
        name="attn_bwd_rest",
    )(sp, p, o, do, own_dp, dh, w)


def norm_stats(h):
    center = h - jnp.mean(h, -1, keepdims=True)
    rstd = lax.rsqrt(jnp.mean(center * center, -1, keepdims=True) + EPS)
    return center * rstd, rstd


def norm_back(dy, xhat, rstd, gain):
    s = dy * gain
    return rstd * (
        s - jnp.mean(s, -1, keepdims=True) - xhat * jnp.mean(s * xhat, -1, keepdims=True)
    )


def gelu_both(u):
    phi = 0.5 + 0.5 * lax.erf(u * 0.7071067811865476)
    pdf = jnp.exp2(u * u * (-0.5 * 1.4426950408889634)) * 0.3989422804014327
    return u * phi, phi + u * pdf


def row8(x):
    return jnp.sum(x.reshape(-1, 8, x.shape[-1]), axis=0)


def ffn_kernel(
    sp_ref,
    x_ref,
    cot_ref,
    o_ref,
    vec_ref,
    bup_ref,
    wo_hbm,
    wu_hbm,
    wd_hbm,
    enc_ref,
    dh_ref,
    do_ref,
    gu_ref,
    gd_ref,
    go_ref,
    sm_ref,
    wo_s,
    wu_s,
    wd_s,
    stage,
    sems,
    g_s,
    gp_s,
    du_s,
    *,
    wo_row,
):
    i = pl.program_id(0)
    me = sp_ref[0]
    tensor, hw = wu_s.shape[0], wo_hbm.shape[1] - wo_row

    @pl.when(i == 0)
    def _():
        work = []
        for j in range(tensor):
            work.append((wo_hbm.at[j, pl.ds(wo_row, hw)], hw, wo_s, j))
        for j in range(tensor):
            work.append((wu_hbm.at[j], 768, wu_s, j))
        for j in range(tensor):
            work.append((wd_hbm.at[j], 768, wd_s, j))

        def copy(n):
            src, r, _, _ = work[n]
            return pltpu.make_async_copy(src, stage.at[n % 3, pl.ds(0, r)], sems.at[n % 3])

        copy(0).start()
        copy(1).start()
        wo_s[...] = jnp.zeros_like(wo_s)
        gu_ref[...] = jnp.zeros_like(gu_ref)
        gd_ref[...] = jnp.zeros_like(gd_ref)
        go_ref[...] = jnp.zeros_like(go_ref)
        sm_ref[...] = jnp.zeros_like(sm_ref)
        for n in range(len(work)):
            if n + 2 < len(work):
                copy(n + 2).start()
            copy(n).wait()
            _, r, dst, j = work[n]
            dst[j, 0:r] = stage[n % 3, 0:r].astype(BF)

    def vec(n):
        return vec_ref[n : n + 1].astype(F32)

    attn = dot(o_ref[0], wo_s[0])
    for j in range(1, tensor):
        attn = attn + dot(o_ref[j], wo_s[j])
    xhat1, rstd1 = norm_stats(x_ref[...].astype(F32) + attn + vec(0))
    y1 = xhat1 * vec(2) + vec(4)
    y1b = y1.astype(BF)
    ffn = jnp.zeros_like(y1)
    for j in range(tensor):
        u = dot(y1b, wu_s[j]) + bup_ref[j : j + 1]
        g, gp = gelu_both(u)
        gb = g.astype(BF)
        g_s[j] = gb
        gp_s[j] = gp
        ffn = ffn + dot(gb, wd_s[j])
    xhat2, rstd2 = norm_stats(y1 + ffn + vec(1))
    enc_ref[...] = (xhat2 * vec(3) + vec(5)).astype(BF)
    dy = cot_ref[...].astype(F32)
    dh2 = norm_back(dy, xhat2, rstd2, vec(3))
    dz = dh2.astype(BF)
    sm_ref[1] += row8(dh2)
    sm_ref[3] += row8(dy * xhat2)
    sm_ref[5] += row8(dy)
    dy1 = dh2
    for j in range(tensor):
        du = (dot(dz, wd_s[j], NT) * gp_s[j]).astype(BF)
        du_s[j] = du
        dy1 = dy1 + dot(du, wu_s[j], NT)
    du_own = du_s[me]
    gu_ref[...] += dot(y1b, du_own, TN)
    gd_ref[...] += dot(dz, g_s[me], TN)
    sm_ref[6] += row8(du_own.astype(F32))
    dh1 = norm_back(dy1, xhat1, rstd1, vec(2))
    dh_ref[...] = dh1
    da = dh1.astype(BF)
    sm_ref[0] += row8(dh1)
    sm_ref[2] += row8(dy1 * xhat1)
    sm_ref[4] += row8(dy1)
    go_ref[...] += dot(da, o_ref[me], TN)
    for j in range(tensor):
        do_ref[j] = dot(da, wo_s[j], NT).astype(BF)


def ffn_block(sp, x, cot, o, vecs, bup, w1, wu, wd, wo_row, blk):
    rows, d = x.shape
    tensor = o.shape[0]
    fl = wu.shape[2]
    row = lambda i, sp: (i, 0)
    grp = lambda i, sp: (0, i, 0)
    const = lambda i, sp: (0, 0)
    return pl.pallas_call(
        lambda *r: ffn_kernel(*r, wo_row=wo_row),
        grid_spec=pltpu.PrefetchScalarGridSpec(
            num_scalar_prefetch=1,
            grid=(rows // blk,),
            in_specs=[
                pl.BlockSpec((blk, d), row),
                pl.BlockSpec((blk, d), row),
                pl.BlockSpec((tensor, blk, 256), grp),
                pl.BlockSpec((8, d), const),
                pl.BlockSpec((tensor, fl), const),
                pl.BlockSpec(memory_space=pl.ANY),
                pl.BlockSpec(memory_space=pl.ANY),
                pl.BlockSpec(memory_space=pl.ANY),
            ],
            out_specs=[
                pl.BlockSpec((blk, d), row),
                pl.BlockSpec((blk, d), row),
                pl.BlockSpec((tensor, blk, 256), grp),
                pl.BlockSpec((d, fl), const, pipeline_mode=pl.Buffered(1)),
                pl.BlockSpec((d, fl), const, pipeline_mode=pl.Buffered(1)),
                pl.BlockSpec((d, 256), const, pipeline_mode=pl.Buffered(1)),
                pl.BlockSpec((8, 8, d), lambda i, sp: (0, 0, 0)),
            ],
            scratch_shapes=[
                pltpu.VMEM((tensor, 256, d), BF),
                pltpu.VMEM((tensor, d, fl), BF),
                pltpu.VMEM((tensor, fl, d), BF),
                pltpu.VMEM((3, 768, 768), F32),
                pltpu.SemaphoreType.DMA((3,)),
                pltpu.VMEM((tensor, blk, fl), BF),
                pltpu.VMEM((tensor, blk, fl), F32),
                pltpu.VMEM((tensor, blk, fl), BF),
            ],
        ),
        out_shape=[
            jax.ShapeDtypeStruct((rows, d), BF),
            jax.ShapeDtypeStruct((rows, d), F32),
            jax.ShapeDtypeStruct((tensor, rows, 256), BF),
            jax.ShapeDtypeStruct((d, fl), F32),
            jax.ShapeDtypeStruct((d, fl), F32),
            jax.ShapeDtypeStruct((d, 256), F32),
            jax.ShapeDtypeStruct((8, 8, d), F32),
        ],
        compiler_params=pltpu.CompilerParams(vmem_limit_bytes=62 * 2**20),
        name="ffn_block",
    )(sp, x, cot, o, vecs, bup, w1, wu, wd)


def gather(shard, n_dp, n_tensor):
    r = shard.shape[0] // n_dp
    piece = lax.dynamic_slice_in_dim(shard, lax.axis_index("dp") * r, r, 0).astype(F32)
    full = lax.all_gather(piece, ("tensor", "dp"), axis=0, tiled=True)
    return full.reshape(n_tensor, shard.shape[0], shard.shape[1])


def make(n_dp, n_tensor):
    def on_device(
        short_tokens,
        short_lengths,
        long_tokens,
        long_lengths,
        w_qkv,
        b_qv,
        w_out,
        res_biases,
        ln_gains,
        ln_shifts,
        w_up,
        b_up,
        w_down,
        short_cotangent,
        long_cotangent,
    ):
        ns, ss, d = short_tokens.shape
        nl, ls, _ = long_tokens.shape
        srows = ns * ss
        rows = srows + nl * ls
        heads, hd = b_qv.shape[1], b_qv.shape[2]
        hw = heads * hd
        blk = ls
        kw = dict(nshort=ns, short_slot=ss, heads=heads, blk=blk)
        me = lax.axis_index("tensor").astype(jnp.int32)
        rest = (me + 1 + jnp.arange(n_tensor - 1, dtype=jnp.int32)) % n_tensor

        w1_own = jnp.concatenate([w_qkv.transpose(0, 2, 1).reshape(3 * hw, d), w_out], 0)
        w1 = gather(w1_own, n_dp, n_tensor)
        wu = gather(w_up, n_dp, n_tensor)
        wd = gather(w_down, n_dp, n_tensor)
        small = jnp.concatenate([b_qv.reshape(2 * hw), b_up.reshape(-1)]).astype(F32)
        small = lax.all_gather(small, "tensor", axis=0)
        bqv = small[:, : 2 * hw].reshape(n_tensor, 2, hw)
        bup = small[:, 2 * hw :]
        one = np.zeros((1, 256 - hw), np.float32)
        one[:, 1 : 1 + 3 * heads] = 1.0
        pad1 = jnp.broadcast_to(jnp.asarray(one), (n_tensor, 256 - hw))
        zero = jnp.zeros((n_tensor, 256 - hw), F32)
        bias = jnp.concatenate(
            [bqv[:, 0], zero, jnp.zeros((n_tensor, hw), F32), pad1, bqv[:, 1], pad1], 1
        ).reshape(n_tensor, 1, 768)

        x = jnp.concatenate([short_tokens.reshape(srows, d), long_tokens.reshape(-1, d)], 0)
        cot = jnp.concatenate(
            [short_cotangent.reshape(srows, d), long_cotangent.reshape(-1, d)], 0
        )
        lens = jnp.concatenate([short_lengths, long_lengths])
        own = me.reshape(1)
        own_first = attn_fwd(
            own, lens, x, w1_own[None], bias, None, w_index=lambda g, sp: 0, **kw
        )
        p, o = attn_fwd(rest, lens, x, w1, bias, own_first, w_index=lambda g, sp: sp[g], **kw)
        vecs = jnp.concatenate([res_biases, ln_gains, ln_shifts, jnp.zeros((2, d), BF)], 0).astype(F32)
        enc, dh, do, gu, gd, go, sm = ffn_block(
            own, x, cot, o, vecs, bup, w1, wu, wd, 3 * hw, 256
        )
        sm = sm.sum(1)
        up_shard = lax.psum_scatter(gu, "dp", scatter_dimension=0, tiled=True)
        down_shard = lax.psum_scatter(gd, "dp", scatter_dimension=0, tiled=True).T
        out_shard = lax.psum_scatter(go[:, :hw], "dp", scatter_dimension=0, tiled=True).T
        small_shard = lax.psum_scatter(sm, "dp", scatter_dimension=1, tiled=True)
        dp_own, gw, gb = bwd_own(own, x, p, o, do, **kw)
        gx = bwd_rest(jnp.concatenate([own, rest]), p, o, do, dp_own, dh, w1, **kw)
        gw = gw.reshape(d, 3, 256)[:, :, :hw].reshape(d, 3 * hw)
        gw = lax.psum_scatter(gw, "dp", scatter_dimension=0, tiled=True)
        gqkv = gw.reshape(-1, 3, hw).transpose(1, 0, 2)
        gb = gb.sum(0).reshape(3, 256)
        gb = jnp.stack([gb[0, :hw], gb[2, :hw]]).reshape(2, heads, hd)
        qv_shard = lax.psum_scatter(gb, "dp", scatter_dimension=2, tiled=True)
        return (
            enc[:srows].reshape(ns, ss, d),
            enc[srows:].reshape(nl, ls, d),
            gx[:srows].reshape(ns, ss, d),
            gx[srows:].reshape(nl, ls, d),
            gqkv,
            qv_shard,
            out_shard,
            small_shard[0:2],
            small_shard[2:4],
            small_shard[4:6],
            up_shard,
            small_shard[6:7],
            down_shard,
        )

    return on_device


def solution(mesh):
    tok = P("dp", None, None)
    return jax.shard_map(
        make(mesh.shape["dp"], mesh.shape["tensor"]),
        mesh=mesh,
        in_specs=(
            tok,
            P("dp"),
            tok,
            P("dp"),
            P(None, None, "tensor"),
            P(None, "tensor", None),
            P("tensor", None),
            P(),
            P(),
            P(),
            P(None, "tensor"),
            P("tensor", None),
            P("tensor", None),
            tok,
            tok,
        ),
        out_specs=(
            tok,
            tok,
            tok,
            tok,
            P(None, "dp", "tensor"),
            P(None, "tensor", "dp"),
            P("tensor", "dp"),
            P(None, "dp"),
            P(None, "dp"),
            P(None, "dp"),
            P("dp", "tensor"),
            P("tensor", "dp"),
            P("tensor", "dp"),
        ),
        check_vma=False,
    )
```

```python
import jax
import jax.numpy as jnp
import numpy as np
from jax import lax
from jax.experimental import pallas as pl
from jax.experimental.pallas import tpu as pltpu
from jax.sharding import PartitionSpec as P

HD = 64
EPS = 1e-12
BF = jnp.bfloat16
F32 = jnp.float32
NT = (((1,), (1,)), ((), ()))
TN = (((0,), (0,)), ((), ()))


def dot(a, b, dims=(((1,), (0,)), ((), ()))):
    return lax.dot_general(a, b, dims, preferred_element_type=F32)


def lanes(width, test):
    lane = lax.broadcasted_iota(jnp.int32, (1, width), 1)
    return jnp.where(test(lane), 1.0, 0.0).astype(F32)


def head_row(h, width, extra):
    w = width * HD

    def test(lane):
        own = (lane >= h * HD) & (lane < (h + 1) * HD)
        if extra:
            own = own | ((lane >= w + 1 + 3 * h) & (lane < w + 4 + 3 * h))
        return own

    return test


def split3(x):
    hi = x.astype(BF).astype(F32)
    rest = x - hi
    mid = rest.astype(BF).astype(F32)
    return hi, mid, rest - mid


def blocks(blk, d, nshort, grid_pos=0):
    return [
        pl.BlockSpec((blk, d), lambda *g: (jnp.minimum(g[grid_pos], nshort - 1), 0)),
        pl.BlockSpec((blk, d), lambda *g: (jnp.maximum(g[grid_pos] - nshort, 0), 0)),
    ]


def fetch(jobs, stage, sems, depth):
    def copy(n):
        src, idx, _ = jobs[n]
        dst = stage.at[n % depth] if idx is None else stage.at[n % depth, idx]
        return pltpu.make_async_copy(src, dst, sems.at[n % depth])

    for n in range(min(depth - 1, len(jobs))):
        copy(n).start()
    for n in range(len(jobs)):
        if n + depth - 1 < len(jobs):
            copy(n + depth - 1).start()
        copy(n).wait()
        jobs[n][2](n % depth)


def attn_fwd_kernel(
    len_ref, place_ref, xs_ref, xl_ref, b_ref, *refs, slot, nshort, short_slot, heads, blk
):
    if slot:
        pieces, (p_ref, o_ref, w_s, x_s, stage, sems) = refs[:8], refs[-6:]
    else:
        w_ref, p_ref, o_ref, w_s, x_s = refs
    hw = heads * HD
    b = pl.program_id(0)
    sub = blk // short_slot
    long0 = nshort // sub

    @pl.when(b == 0)
    def _():
        if slot:
            copies = [
                pltpu.make_async_copy(pieces[n].at[slot - 1], stage.at[n], sems.at[n])
                for n in range(8)
            ]
            for c in copies:
                c.start()
            w_s[...] = jnp.zeros_like(w_s)
            r = stage.shape[1]
            for n in range(8):
                copies[n].wait()
                row = place_ref[1, n]

                @pl.when(row >= 0)
                def _():
                    w_s[pl.ds(pl.multiple_of(row, 32), r)] = stage[n].astype(BF)

        else:
            w_s[...] = jnp.zeros_like(w_s)
            for c in range(3):
                w_s[256 * c : 256 * c + hw] = w_ref[c * hw : (c + 1) * hw]

    @pl.when(b < long0)
    def _():
        x_s[...] = xs_ref[...]

    @pl.when(b >= long0)
    def _():
        x_s[...] = xl_ref[...]

    p_ref[0] = (dot(x_s[...], w_s[...], NT) + b_ref[...]).astype(BF)

    def pair(row, rows, length):
        sl = pl.ds(row, rows)
        pos = lax.broadcasted_iota(jnp.int32, (rows, 1), 0)
        hidden = jnp.where(pos < length, 0.0, -1e30)
        at_mask = lanes(256, lambda l: l == hw)
        q = (p_ref[0, sl, 0:256].astype(F32) * 0.125 + at_mask).astype(BF)
        k = (p_ref[0, sl, 256:512].astype(F32) + hidden * at_mask).astype(BF)
        v = p_ref[0, sl, 512:768]
        p_ref[0, sl, 256:512] = k
        out = jnp.zeros((rows, 256), F32)
        ext = jnp.zeros((rows, 256), F32)
        for h in range(heads):
            own = lanes(256, head_row(h, heads, False))
            s = dot(q * (own + at_mask).astype(BF), k, NT)
            m = jnp.max(s, axis=1, keepdims=True)
            e = jnp.exp(s - m)
            total = jnp.sum(e, axis=1, keepdims=True)
            a = (e * (1.0 / total)).astype(BF)
            out = out + dot(a, v * own.astype(BF))
            for i, part in enumerate(split3(-(m + jnp.log(total)))):
                ext = ext + part * lanes(256, lambda l: l == hw + 1 + 3 * h + i)
        p_ref[0, sl, 0:256] = (q.astype(F32) + ext).astype(BF)
        o_ref[0, sl] = out.astype(BF)

    @pl.when(b < long0)
    def _():
        for i in range(sub):
            pair(i * short_slot, short_slot, len_ref[b * sub + i])

    @pl.when(b >= long0)
    def _():
        pair(0, blk, len_ref[nshort + b - long0])


def attn_fwd(slot, lens, place, xs, xl, w, bias, prev, nshort, short_slot, heads, blk, slots):
    rows, d = xs.shape[0] + xl.shape[0], xs.shape[1]
    in_specs = blocks(blk, d, xs.shape[0] // blk) + [pl.BlockSpec((1, 768), lambda b, *_: (0, 0))]
    args = [xs, xl, bias]
    scratch = [pltpu.VMEM((768, d), BF), pltpu.VMEM((blk, d), BF)]
    aliases = {}
    if slot:
        in_specs += [pl.BlockSpec(memory_space=pl.ANY)] * 10
        args += list(w) + list(prev)
        aliases = {13: 0, 14: 1}
        r = w[0].shape[1]
        scratch += [pltpu.VMEM((8, r, d), F32), pltpu.SemaphoreType.DMA((8,))]
    else:
        in_specs.append(pl.BlockSpec(w.shape, lambda b, *_: (0, 0)))
        args.append(w)
    return pl.pallas_call(
        lambda *r: attn_fwd_kernel(
            *r, slot=slot, nshort=nshort, short_slot=short_slot, heads=heads, blk=blk
        ),
        grid_spec=pltpu.PrefetchScalarGridSpec(
            num_scalar_prefetch=2,
            grid=(rows // blk,),
            in_specs=in_specs,
            out_specs=[
                pl.BlockSpec((1, blk, 768), lambda b, *_: (slot, b, 0)),
                pl.BlockSpec((1, blk, 256), lambda b, *_: (slot, b, 0)),
            ],
            scratch_shapes=scratch,
        ),
        out_shape=[
            jax.ShapeDtypeStruct((slots, rows, 768), BF),
            jax.ShapeDtypeStruct((slots, rows, 256), BF),
        ],
        input_output_aliases=aliases,
        compiler_params=pltpu.CompilerParams(vmem_limit_bytes=60 * 2**20),
        cost_estimate=pl.CostEstimate(flops=14 * 10**9, bytes_accessed=2**23, transcendentals=0),
        name="attn_fwd",
    )(lens, place, *args)


def attn_bwd_pair(refs, sl, rows, heads):
    p_ref, o_ref, do_ref = refs
    hw = heads * HD
    q, k, v = p_ref[0, sl, 0:256], p_ref[0, sl, 256:512], p_ref[0, sl, 512:768]
    do = do_ref[0, sl]
    do32 = do.astype(F32)
    prod = do32 * o_ref[0, sl].astype(F32)
    ext = do32
    for h in range(heads):
        own = lanes(256, head_row(h, heads, False))
        delta = jnp.sum(prod * own, axis=1, keepdims=True)
        for i, part in enumerate(split3(-delta)):
            ext = ext + part * lanes(256, lambda l: l == hw + 1 + 3 * h + i)
    do_ext = ext.astype(BF)
    kt = k.T
    at_mask = lanes(256, lambda l: l == hw)
    dk = jnp.zeros((rows, 256), F32)
    dv = jnp.zeros((rows, 256), F32)
    dqs = []
    for h in range(heads):
        row = lanes(256, head_row(h, heads, True))
        qh = q * (row + at_mask).astype(BF)
        doh = do_ext * row.astype(BF)
        p = jnp.exp(dot(k, qh, NT))
        ds = (p * dot(v, doh, NT)).astype(BF)
        dv = dv + dot(p.astype(BF), doh)
        dk = dk + dot(ds, qh)
        dqs.append(dot(kt[h * HD : (h + 1) * HD], ds))
    dqs.append(jnp.zeros((256 - hw, rows), F32))
    dq = jnp.concatenate(dqs, 0).T * 0.125
    real = lanes(256, lambda l: l < hw)
    return dq.astype(BF), (dk * real).astype(BF), (dv * real).astype(BF)


def over_pairs(b, refs, dst, *, nshort, short_slot, heads, blk):
    sub = blk // short_slot
    long0 = nshort // sub

    def one(row, rows):
        sl = pl.ds(row, rows)
        for c, val in enumerate(attn_bwd_pair(refs, sl, rows, heads)):
            dst(sl, c, val)

    @pl.when(b < long0)
    def _():
        for i in range(sub):
            one(i * short_slot, short_slot)

    @pl.when(b >= long0)
    def _():
        one(0, blk)


def bwd_own_kernel(xs_ref, xl_ref, p_ref, o_ref, do_ref, dp_ref, gw_ref, gb_ref, **kw):
    b = pl.program_id(0)
    long0 = kw["nshort"] * kw["short_slot"] // kw["blk"]

    def dst(sl, c, val):
        dp_ref[sl, 256 * c : 256 * (c + 1)] = val

    over_pairs(b, (p_ref, o_ref, do_ref), dst, **kw)

    @pl.when(b == 0)
    def _():
        gw_ref[...] = jnp.zeros_like(gw_ref)
        gb_ref[...] = jnp.zeros_like(gb_ref)

    @pl.when(b < long0)
    def _():
        gw_ref[...] += dot(xs_ref[...], dp_ref[...], TN)

    @pl.when(b >= long0)
    def _():
        gw_ref[...] += dot(xl_ref[...], dp_ref[...], TN)

    gb_ref[...] += jnp.sum(dp_ref[...].astype(F32).reshape(-1, 8, 768), axis=0)


def bwd_own(xs, xl, p, o, do, blk, **kw):
    rows, d = xs.shape[0] + xl.shape[0], xs.shape[1]
    return pl.pallas_call(
        lambda *r: bwd_own_kernel(*r, blk=blk, **kw),
        grid=(rows // blk,),
        in_specs=blocks(blk, d, xs.shape[0] // blk)
        + [
            pl.BlockSpec((1, blk, 768), lambda b: (0, b, 0)),
            pl.BlockSpec((1, blk, 256), lambda b: (0, b, 0)),
            pl.BlockSpec((1, blk, 256), lambda b: (0, b, 0)),
        ],
        out_specs=[
            pl.BlockSpec((blk, 768), lambda b: (b, 0)),
            pl.BlockSpec((d, 768), lambda b: (0, 0)),
            pl.BlockSpec((8, 768), lambda b: (0, 0)),
        ],
        out_shape=[
            jax.ShapeDtypeStruct((rows, 768), BF),
            jax.ShapeDtypeStruct((d, 768), F32),
            jax.ShapeDtypeStruct((8, 768), F32),
        ],
        compiler_params=pltpu.CompilerParams(vmem_limit_bytes=60 * 2**20),
        cost_estimate=pl.CostEstimate(flops=18 * 10**9, bytes_accessed=2**23, transcendentals=0),
        name="attn_bwd_own",
    )(xs, xl, p, o, do)


def bwd_rest_kernel(
    place_ref, p_ref, o_ref, do_ref, own_ref, dh_ref, w_hbm, *refs, **kw
):
    pieces, (gs_ref, gl_ref, dp_s, w_s, stage, sems, sem) = refs[:8], refs[8:]
    b, g = pl.program_id(0), pl.program_id(1)
    slots = w_s.shape[0]
    hw = kw["heads"] * HD
    long0 = kw["nshort"] * kw["short_slot"] // kw["blk"]

    @pl.when((b == 0) & (g == 0))
    def _():
        own = [
            pltpu.make_async_copy(
                w_hbm.at[pl.ds(c * hw, hw)], w_s.at[0, pl.ds(256 * c, hw)], sem.at[c]
            )
            for c in range(3)
        ]
        w_s[...] = jnp.zeros_like(w_s)
        for c in own:
            c.start()

        def store(n):
            def put(at):
                row = place_ref[1, n]

                @pl.when(row >= 0)
                def _():
                    for j in range(slots - 1):
                        w_s[j + 1, pl.ds(pl.multiple_of(row, 32), stage.shape[2])] = stage[
                            at, j
                        ].astype(BF)

            return put

        fetch([(pieces[n], None, store(n)) for n in range(8)], stage, sems, 3)
        for c in own:
            c.wait()

    @pl.when(g == 0)
    def _():
        dp_s[0] = own_ref[...]

    def dst(sl, c, val):
        dp_s[g + 1, sl, 256 * c : 256 * (c + 1)] = val

    over_pairs(b, (p_ref, o_ref, do_ref), dst, **kw)

    @pl.when(g == slots - 2)
    def _():
        acc = dh_ref[...]
        for j in range(slots):
            acc = acc + dot(dp_s[j], w_s[j])

        @pl.when(b < long0)
        def _():
            gs_ref[...] = acc

        @pl.when(b >= long0)
        def _():
            gl_ref[...] = acc


def bwd_rest(place, p, o, do, own_dp, dh, w_own, pieces, srows, blk, **kw):
    slots, rows, _ = p.shape
    d = dh.shape[1]
    r = pieces[0].shape[1]

    def grp_map(b, g, *_):
        return (g + 1, b, 0)

    return pl.pallas_call(
        lambda *r: bwd_rest_kernel(*r, blk=blk, **kw),
        grid_spec=pltpu.PrefetchScalarGridSpec(
            num_scalar_prefetch=1,
            grid=(rows // blk, slots - 1),
            in_specs=[
                pl.BlockSpec((1, blk, 768), grp_map),
                pl.BlockSpec((1, blk, 256), grp_map),
                pl.BlockSpec((1, blk, 256), grp_map),
                pl.BlockSpec((blk, 768), lambda b, g, *_: (b, 0)),
                pl.BlockSpec((blk, d), lambda b, g, *_: (b, 0)),
            ]
            + [pl.BlockSpec(memory_space=pl.ANY)] * 9,
            out_specs=blocks(blk, d, srows // blk),
            scratch_shapes=[
                pltpu.VMEM((slots, blk, 768), BF),
                pltpu.VMEM((slots, 768, d), BF),
                pltpu.VMEM((3, slots - 1, r, d), F32),
                pltpu.SemaphoreType.DMA((3,)),
                pltpu.SemaphoreType.DMA((3,)),
            ],
        ),
        out_shape=[
            jax.ShapeDtypeStruct((srows, d), F32),
            jax.ShapeDtypeStruct((rows - srows, d), F32),
        ],
        compiler_params=pltpu.CompilerParams(vmem_limit_bytes=60 * 2**20),
        cost_estimate=pl.CostEstimate(flops=50 * 10**9, bytes_accessed=2**23, transcendentals=0),
        name="attn_bwd_rest",
    )(place, p, o, do, own_dp, dh, w_own, *pieces)


def norm_stats(h):
    center = h - jnp.mean(h, -1, keepdims=True)
    rstd = lax.rsqrt(jnp.mean(center * center, -1, keepdims=True) + EPS)
    return center * rstd, rstd


def norm_back(dy, xhat, rstd, gain):
    s = dy * gain
    return rstd * (
        s - jnp.mean(s, -1, keepdims=True) - xhat * jnp.mean(s * xhat, -1, keepdims=True)
    )


def gelu_both(u):
    phi = 0.5 + 0.5 * lax.erf(u * 0.7071067811865476)
    pdf = jnp.exp2(u * u * (-0.5 * 1.4426950408889634)) * 0.3989422804014327
    return u * phi, phi + u * pdf


def row8(x):
    return jnp.sum(x.reshape(-1, 8, x.shape[-1]), axis=0)


def ffn_kernel(place_ref, *refs, long0, hw):
    (xs_ref, xl_ref, cs_ref, cl_ref, o_ref, vec_ref, bup_ref, w1_hbm, wu_hbm, wd_hbm) = refs[:10]
    w1_pieces, wu_pieces, wd_pieces = refs[10:18], refs[18:26], refs[26:34]
    (es_ref, el_ref, dh_ref, do_ref, gall_ref) = refs[34:39]
    (wo_s, wu_s, wd_s, stage, sems, sem, g_s, gp_s, du_s, sm_s, x_s, c_s) = refs[39:]
    i = pl.program_id(0)
    slots, d, fl = wu_s.shape
    r = stage.shape[2]

    @pl.when(i == 0)
    def _():
        wo_s[...] = jnp.zeros_like(wo_s)
        own = [
            pltpu.make_async_copy(wu_hbm, wu_s.at[0], sem.at[0]),
            pltpu.make_async_copy(wd_hbm, wd_s.at[0], sem.at[1]),
            pltpu.make_async_copy(
                w1_hbm.at[pl.ds(3 * hw, hw)], wo_s.at[0, pl.ds(0, hw)], sem.at[2]
            ),
        ]
        for c in own:
            c.start()

        def store(dst, n):
            def put(at):
                row = pl.multiple_of(place_ref[0, n], 32)
                for j in range(slots - 1):
                    dst[j + 1, pl.ds(row, r)] = stage[at, j].astype(BF)

            return put

        def store_out(n):
            def put(at):
                row = place_ref[2, n]

                @pl.when(row >= 0)
                def _():
                    for j in range(slots - 1):
                        wo_s[j + 1, pl.ds(pl.multiple_of(row, 32), r)] = stage[at, j].astype(BF)

            return put

        jobs = [(w1_pieces[n], None, store_out(n)) for n in range(8)]
        jobs += [(wu_pieces[n], None, store(wu_s, n)) for n in range(8)]
        jobs += [(wd_pieces[n], None, store(wd_s, n)) for n in range(8)]
        fetch(jobs, stage, sems, 4)
        gall_ref[...] = jnp.zeros_like(gall_ref)
        sm_s[...] = jnp.zeros_like(sm_s)
        for c in own:
            c.wait()

    @pl.when(i < long0)
    def _():
        x_s[...] = xs_ref[...]
        c_s[...] = cs_ref[...]

    @pl.when(i >= long0)
    def _():
        x_s[...] = xl_ref[...]
        c_s[...] = cl_ref[...]

    def vec(n):
        return vec_ref[n : n + 1].astype(F32)

    attn = dot(o_ref[0], wo_s[0])
    for j in range(1, slots):
        attn = attn + dot(o_ref[j], wo_s[j])
    xhat1, rstd1 = norm_stats(x_s[...].astype(F32) + attn + vec(0))
    y1 = xhat1 * vec(2) + vec(4)
    y1b = y1.astype(BF)
    ffn = jnp.zeros_like(y1)
    for j in range(slots):
        u = dot(y1b, wu_s[j]) + bup_ref[j : j + 1]
        g, gp = gelu_both(u)
        gb = g.astype(BF)
        g_s[j] = gb
        gp_s[j] = gp
        ffn = ffn + dot(gb, wd_s[j])
    xhat2, rstd2 = norm_stats(y1 + ffn + vec(1))
    enc = (xhat2 * vec(3) + vec(5)).astype(BF)

    @pl.when(i < long0)
    def _():
        es_ref[...] = enc

    @pl.when(i >= long0)
    def _():
        el_ref[...] = enc

    dy = c_s[...].astype(F32)
    dh2 = norm_back(dy, xhat2, rstd2, vec(3))
    dz = dh2.astype(BF)
    sm_s[1] += row8(dh2)
    sm_s[3] += row8(dy * xhat2)
    sm_s[5] += row8(dy)
    dy1 = dh2
    for j in range(slots):
        du = (dot(dz, wd_s[j], NT) * gp_s[j]).astype(BF)
        du_s[j] = du
        dy1 = dy1 + dot(du, wu_s[j], NT)
    gall_ref[:, 0:fl] += dot(y1b, du_s[0], TN)
    gall_ref[:, fl : 2 * fl] += dot(dz, g_s[0], TN)
    sm_s[6] += row8(du_s[0].astype(F32))
    dh1 = norm_back(dy1, xhat1, rstd1, vec(2))
    dh_ref[...] = dh1
    da = dh1.astype(BF)
    sm_s[0] += row8(dh1)
    sm_s[2] += row8(dy1 * xhat1)
    sm_s[4] += row8(dy1)
    gall_ref[:, 2 * fl : 2 * fl + 256] += dot(da, o_ref[0], TN)
    for j in range(slots):
        do_ref[j] = dot(da, wo_s[j], NT).astype(BF)

    @pl.when(i == pl.num_programs(0) - 1)
    def _():
        small = jnp.sum(sm_s[...], axis=1)
        small = jnp.concatenate([small, jnp.zeros((120, d), F32)], 0)
        gall_ref[:, 2 * fl + 256 :] = small.T


def ffn_block(place, xs, xl, cs, cl, o, vecs, bup, own, pieces, hw, blk):
    srows, d = xs.shape
    rows = srows + xl.shape[0]
    slots = o.shape[0]
    fl = own[1].shape[1]
    r = pieces[0].shape[1]
    long0 = srows // blk
    row = lambda i, *_: (i, 0)
    grp = lambda i, *_: (0, i, 0)
    const = lambda i, *_: (0, 0)
    return pl.pallas_call(
        lambda *r: ffn_kernel(*r, long0=long0, hw=hw),
        grid_spec=pltpu.PrefetchScalarGridSpec(
            num_scalar_prefetch=1,
            grid=(rows // blk,),
            in_specs=blocks(blk, d, long0)
            + blocks(blk, d, long0)
            + [
                pl.BlockSpec((slots, blk, 256), grp),
                pl.BlockSpec((8, d), const),
                pl.BlockSpec((slots, fl), const),
            ]
            + [pl.BlockSpec(memory_space=pl.ANY)] * 27,
            out_specs=blocks(blk, d, long0)
            + [
                pl.BlockSpec((blk, d), row),
                pl.BlockSpec((slots, blk, 256), grp),
                pl.BlockSpec((d, 2 * fl + 384), const, pipeline_mode=pl.Buffered(1)),
            ],
            scratch_shapes=[
                pltpu.VMEM((slots, 256, d), BF),
                pltpu.VMEM((slots, d, fl), BF),
                pltpu.VMEM((slots, fl, d), BF),
                pltpu.VMEM((4, slots - 1, r, d), F32),
                pltpu.SemaphoreType.DMA((4,)),
                pltpu.SemaphoreType.DMA((3,)),
                pltpu.VMEM((slots, blk, fl), BF),
                pltpu.VMEM((slots, blk, fl), F32),
                pltpu.VMEM((slots, blk, fl), BF),
                pltpu.VMEM((8, 8, d), F32),
                pltpu.VMEM((blk, d), BF),
                pltpu.VMEM((blk, d), BF),
            ],
        ),
        out_shape=[
            jax.ShapeDtypeStruct((srows, d), BF),
            jax.ShapeDtypeStruct((rows - srows, d), BF),
            jax.ShapeDtypeStruct((rows, d), F32),
            jax.ShapeDtypeStruct((slots, rows, 256), BF),
            jax.ShapeDtypeStruct((d, 2 * fl + 384), F32),
        ],
        compiler_params=pltpu.CompilerParams(vmem_limit_bytes=62 * 2**20),
        cost_estimate=pl.CostEstimate(flops=80 * 10**9, bytes_accessed=2**25, transcendentals=0),
        name="ffn_block",
    )(place, xs, xl, cs, cl, o, vecs, bup, *own, *pieces)


class Wires:
    def __init__(self, n_dp, n_tensor):
        self.n_dp, self.n_tensor = n_dp, n_tensor
        self.first = [(i, i ^ (4 if i & 1 else 2)) for i in range(n_dp)]
        self.second = [(i, i ^ (2 if i & 1 else 4)) for i in range(n_dp)]
        self.pair = [(i, i ^ 1) for i in range(n_dp)]
        me = lax.axis_index("dp")
        odd = (me & 1).astype(jnp.int32)
        a, b = 2 + 2 * odd, 4 - 2 * odd
        masks = [0, a, b, 6, 1, 1 ^ b, 1 ^ a, 7]
        self.low = (me & 7).astype(jnp.int32)
        self.source = jnp.stack([jnp.asarray(self.low ^ m, jnp.int32) for m in masks])

    def piece(self, shard):
        extra = self.n_dp // 8
        r = shard.shape[0] // self.n_dp
        at = (self.low * extra + lax.axis_index("dp") // 8) * r
        return lax.dynamic_slice_in_dim(shard, at, r, 0).astype(F32)

    def along_tensor(self, piece):
        n = self.n_tensor
        return [
            lax.ppermute(piece, "tensor", [(i, (i + s) % n) for i in range(n)]) for s in range(1, n)
        ]

    def whole_eighth(self, z):
        if self.n_dp == 8:
            return z
        groups = [[g + 8 * e for e in range(self.n_dp // 8)] for g in range(8)]
        return lax.all_gather(z, "dp", axis=1, tiled=True, axis_index_groups=groups)

    def first_hop(self, z):
        return lax.ppermute(z, "dp", self.first), lax.ppermute(z, "dp", self.second)

    def second_hop(self, a):
        return lax.ppermute(a, "dp", self.second)

    def to_pair(self, x):
        return lax.ppermute(x, "dp", self.pair)


def after(x, *others):
    return lax.optimization_barrier((x, *others))[0]


def make(n_dp, n_tensor):
    def on_device(
        short_tokens,
        short_lengths,
        long_tokens,
        long_lengths,
        w_qkv,
        b_qv,
        w_out,
        res_biases,
        ln_gains,
        ln_shifts,
        w_up,
        b_up,
        w_down,
        short_cotangent,
        long_cotangent,
    ):
        ns, ss, d = short_tokens.shape
        nl, ls, _ = long_tokens.shape
        srows = ns * ss
        heads, hd = b_qv.shape[1], b_qv.shape[2]
        hw = heads * hd
        blk = ls
        kw = dict(nshort=ns, short_slot=ss, heads=heads, blk=blk)
        wires = Wires(n_dp, n_tensor)
        r = w_up.shape[0] // 8

        w1_own = jnp.concatenate([w_qkv.transpose(0, 2, 1).reshape(3 * hw, d), w_out], 0)
        tail = jnp.zeros((d - 2 * hw,), F32)
        small = jnp.stack([b_up[0].astype(F32), jnp.concatenate([b_qv.reshape(2 * hw).astype(F32), tail])])
        small = jnp.concatenate([small, jnp.zeros((6, d), F32)], 0)
        piece = wires.piece(w1_own)
        pr = piece.shape[0]
        z = wires.along_tensor(jnp.concatenate([small, piece], 0))
        row = wires.source * r
        c = row // hw
        place = jnp.stack(
            [row, jnp.where(c < 3, c * 256 + row - c * hw, -1), jnp.where(c < 3, -1, row - 3 * hw)]
        )

        one = np.zeros((256 - hw,), np.float32)
        one[1 : 1 + 3 * heads] = 1.0
        one = jnp.asarray(one)

        def bias_of(sm):
            zero = jnp.zeros((256 - hw,), F32)
            none = jnp.zeros((hw,), F32)
            return jnp.concatenate([sm[1, :hw], zero, none, one, sm[1, hw : 2 * hw], one])[None]

        xs, xl = short_tokens.reshape(srows, d), long_tokens.reshape(-1, d)
        cs, cl = short_cotangent.reshape(srows, d), long_cotangent.reshape(-1, d)
        lens = jnp.concatenate([short_lengths, long_lengths])
        po = attn_fwd(0, lens, place, xs, xl, w1_own, bias_of(small), None, slots=n_tensor, **kw)

        zu = wires.along_tensor(after(wires.piece(w_up), *z))
        zd = wires.along_tensor(after(wires.piece(w_down), *zu))
        t1 = wires.whole_eighth(jnp.stack([x[8:] for x in z]))
        a1, b1 = wires.first_hop(t1)
        c1 = wires.second_hop(a1)
        w1 = [t1, a1, b1, c1]
        w1 += [wires.to_pair(x) for x in w1]
        tu = wires.whole_eighth(after(jnp.stack(zu), c1))
        au, bu = wires.first_hop(tu)
        po = attn_fwd(1, lens, place, xs, xl, w1, bias_of(z[0]), po, slots=n_tensor, **kw)
        cu = wires.second_hop(au)
        wu = [tu, au, bu, cu]
        wu += [wires.to_pair(x) for x in wu]
        td = wires.whole_eighth(after(jnp.stack(zd), cu))
        ad, bd = wires.first_hop(td)
        for s in range(2, n_tensor):
            po = attn_fwd(s, lens, place, xs, xl, w1, bias_of(z[s - 1]), po, slots=n_tensor, **kw)
        cd = wires.second_hop(ad)
        wd = [td, ad, bd, cd]
        wd += [wires.to_pair(x) for x in wd]
        p, o = po
        bup = jnp.stack([x[0] for x in [small] + z])
        vecs = jnp.concatenate([res_biases, ln_gains, ln_shifts, jnp.zeros((2, d), BF)], 0).astype(F32)
        es, el, dh, do, gall = ffn_block(
            place, xs, xl, cs, cl, o, vecs, bup, [w1_own, w_up, w_down], w1 + wu + wd, hw, 256
        )
        fl = w_up.shape[1]
        gall = lax.psum_scatter(gall, "dp", scatter_dimension=0, tiled=True)
        small_shard = gall[:, 2 * fl + 256 : 2 * fl + 264].T
        dp_own, gw, gb = bwd_own(xs, xl, p, o, do, **kw)
        gs, gl = bwd_rest(place, p, o, do, dp_own, dh, w1_own, w1, srows, **kw)
        gb = gb.sum(0).reshape(3, 256)
        gb = jnp.stack([gb[0, :hw], gb[2, :hw]]).reshape(2 * heads, n_dp, hd // n_dp)
        gb = gb.transpose(1, 0, 2).reshape(n_dp, 1, -1)
        gw = lax.dynamic_update_slice(gw.reshape(n_dp, d // n_dp, 768), gb, (0, 0, hw))
        gw = lax.psum_scatter(gw.reshape(d, 768), "dp", scatter_dimension=0, tiled=True)
        gqkv = gw.reshape(-1, 3, 256)[:, :, :hw].transpose(1, 0, 2)
        qv_shard = gw[0, hw : hw + 2 * hw // n_dp].reshape(2, heads, hd // n_dp)
        return (
            es.reshape(ns, ss, d),
            el.reshape(nl, ls, d),
            gs.reshape(ns, ss, d),
            gl.reshape(nl, ls, d),
            gqkv,
            qv_shard,
            gall[:, 2 * fl : 2 * fl + hw].T,
            small_shard[0:2],
            small_shard[2:4],
            small_shard[4:6],
            gall[:, :fl],
            small_shard[6:7],
            gall[:, fl : 2 * fl].T,
        )

    return on_device


def solution(mesh):
    tok = P("dp", None, None)
    return jax.shard_map(
        make(mesh.shape["dp"], mesh.shape["tensor"]),
        mesh=mesh,
        in_specs=(
            tok,
            P("dp"),
            tok,
            P("dp"),
            P(None, None, "tensor"),
            P(None, "tensor", None),
            P("tensor", None),
            P(),
            P(),
            P(),
            P(None, "tensor"),
            P("tensor", None),
            P("tensor", None),
            tok,
            tok,
        ),
        out_specs=(
            tok,
            tok,
            tok,
            tok,
            P(None, "dp", "tensor"),
            P(None, "tensor", "dp"),
            P("tensor", "dp"),
            P(None, "dp"),
            P(None, "dp"),
            P(None, "dp"),
            P("dp", "tensor"),
            P("tensor", "dp"),
            P("tensor", "dp"),
        ),
        check_vma=False,
    )
```

```python
import jax
import jax.numpy as jnp
import numpy as np
from jax import lax
from jax.experimental import pallas as pl
from jax.experimental.pallas import tpu as pltpu
from jax.sharding import PartitionSpec as P

HD = 64
EPS = 1e-12
BF = jnp.bfloat16
F32 = jnp.float32
NT = (((1,), (1,)), ((), ()))
TN = (((0,), (0,)), ((), ()))


def dot(a, b, dims=(((1,), (0,)), ((), ()))):
    return lax.dot_general(a, b, dims, preferred_element_type=F32)


def lanes(width, test):
    lane = lax.broadcasted_iota(jnp.int32, (1, width), 1)
    return jnp.where(test(lane), 1.0, 0.0).astype(F32)


def head_row(h, width, extra):
    w = width * HD

    def test(lane):
        own = (lane >= h * HD) & (lane < (h + 1) * HD)
        if extra:
            own = own | ((lane >= w + 1 + 3 * h) & (lane < w + 4 + 3 * h))
        return own

    return test


def split3(x):
    hi = x.astype(BF).astype(F32)
    rest = x - hi
    mid = rest.astype(BF).astype(F32)
    return hi, mid, rest - mid


def blocks(blk, d, nshort, grid_pos=0):
    return [
        pl.BlockSpec((blk, d), lambda *g: (jnp.minimum(g[grid_pos], nshort - 1), 0)),
        pl.BlockSpec((blk, d), lambda *g: (jnp.maximum(g[grid_pos] - nshort, 0), 0)),
    ]


def fetch(jobs, stage, sems, depth):
    def copy(n):
        src, idx, _ = jobs[n]
        dst = stage.at[n % depth] if idx is None else stage.at[n % depth, idx]
        return pltpu.make_async_copy(src, dst, sems.at[n % depth])

    for n in range(min(depth - 1, len(jobs))):
        copy(n).start()
    for n in range(len(jobs)):
        if n + depth - 1 < len(jobs):
            copy(n + depth - 1).start()
        copy(n).wait()
        jobs[n][2](n % depth)


def attn_fwd_kernel(
    len_ref, place_ref, xs_ref, xl_ref, b_ref, *refs, slot, nshort, short_slot, heads, blk
):
    if slot:
        pieces, (p_ref, o_ref, w_s, x_s, stage, sems) = refs[:8], refs[-6:]
    else:
        w_ref, p_ref, o_ref, w_s, x_s = refs
    hw = heads * HD
    b = pl.program_id(0)
    sub = blk // short_slot
    long0 = nshort // sub

    @pl.when(b == 0)
    def _():
        if slot:
            copies = [
                pltpu.make_async_copy(pieces[n].at[slot - 1], stage.at[n], sems.at[n])
                for n in range(8)
            ]
            for c in copies:
                c.start()
            w_s[...] = jnp.zeros_like(w_s)
            r = stage.shape[1]
            for n in range(8):
                copies[n].wait()
                row = place_ref[1, n]

                @pl.when(row >= 0)
                def _():
                    w_s[pl.ds(pl.multiple_of(row, 32), r)] = stage[n].astype(BF)

        else:
            w_s[...] = jnp.zeros_like(w_s)
            for c in range(3):
                w_s[256 * c : 256 * c + hw] = w_ref[c * hw : (c + 1) * hw]

    @pl.when(b < long0)
    def _():
        x_s[...] = xs_ref[...]

    @pl.when(b >= long0)
    def _():
        x_s[...] = xl_ref[...]

    p_ref[0] = (dot(x_s[...], w_s[...], NT) + b_ref[...]).astype(BF)

    def pair(row, rows, length):
        sl = pl.ds(row, rows)
        pos = lax.broadcasted_iota(jnp.int32, (rows, 1), 0)
        hidden = jnp.where(pos < length, 0.0, -1e30)
        at_mask = lanes(256, lambda l: l == hw)
        q = (p_ref[0, sl, 0:256].astype(F32) * 0.125 + at_mask).astype(BF)
        k = (p_ref[0, sl, 256:512].astype(F32) + hidden * at_mask).astype(BF)
        v = p_ref[0, sl, 512:768]
        p_ref[0, sl, 256:512] = k
        out = jnp.zeros((rows, 256), F32)
        ext = jnp.zeros((rows, 256), F32)
        for h in range(heads):
            own = lanes(256, head_row(h, heads, False))
            s = dot(q * (own + at_mask).astype(BF), k, NT)
            m = jnp.max(s, axis=1, keepdims=True)
            e = jnp.exp(s - m)
            total = jnp.sum(e, axis=1, keepdims=True)
            a = (e * (1.0 / total)).astype(BF)
            out = out + dot(a, v * own.astype(BF))
            for i, part in enumerate(split3(-(m + jnp.log(total)))):
                ext = ext + part * lanes(256, lambda l: l == hw + 1 + 3 * h + i)
        p_ref[0, sl, 0:256] = (q.astype(F32) + ext).astype(BF)
        o_ref[0, sl] = out.astype(BF)

    @pl.when(b < long0)
    def _():
        for i in range(sub):
            pair(i * short_slot, short_slot, len_ref[b * sub + i])

    @pl.when(b >= long0)
    def _():
        pair(0, blk, len_ref[nshort + b - long0])


def attn_fwd(slot, lens, place, xs, xl, w, bias, prev, nshort, short_slot, heads, blk, slots):
    rows, d = xs.shape[0] + xl.shape[0], xs.shape[1]
    in_specs = blocks(blk, d, xs.shape[0] // blk) + [pl.BlockSpec((1, 768), lambda b, *_: (0, 0))]
    args = [xs, xl, bias]
    scratch = [pltpu.VMEM((768, d), BF), pltpu.VMEM((blk, d), BF)]
    aliases = {}
    if slot:
        in_specs += [pl.BlockSpec(memory_space=pl.ANY)] * 10
        args += list(w) + list(prev)
        aliases = {13: 0, 14: 1}
        r = w[0].shape[1]
        scratch += [pltpu.VMEM((8, r, d), F32), pltpu.SemaphoreType.DMA((8,))]
    else:
        in_specs.append(pl.BlockSpec(w.shape, lambda b, *_: (0, 0)))
        args.append(w)
    return pl.pallas_call(
        lambda *r: attn_fwd_kernel(
            *r, slot=slot, nshort=nshort, short_slot=short_slot, heads=heads, blk=blk
        ),
        grid_spec=pltpu.PrefetchScalarGridSpec(
            num_scalar_prefetch=2,
            grid=(rows // blk,),
            in_specs=in_specs,
            out_specs=[
                pl.BlockSpec((1, blk, 768), lambda b, *_: (slot, b, 0)),
                pl.BlockSpec((1, blk, 256), lambda b, *_: (slot, b, 0)),
            ],
            scratch_shapes=scratch,
        ),
        out_shape=[
            jax.ShapeDtypeStruct((slots, rows, 768), BF),
            jax.ShapeDtypeStruct((slots, rows, 256), BF),
        ],
        input_output_aliases=aliases,
        compiler_params=pltpu.CompilerParams(vmem_limit_bytes=60 * 2**20),
        cost_estimate=pl.CostEstimate(flops=14 * 10**9, bytes_accessed=2**23, transcendentals=0),
        name="attn_fwd",
    )(lens, place, *args)


def attn_bwd_pair(refs, sl, rows, heads):
    p_ref, o_ref, do_ref = refs
    hw = heads * HD
    q, k, v = p_ref[0, sl, 0:256], p_ref[0, sl, 256:512], p_ref[0, sl, 512:768]
    do = do_ref[0, sl]
    do32 = do.astype(F32)
    prod = do32 * o_ref[0, sl].astype(F32)
    ext = do32
    for h in range(heads):
        own = lanes(256, head_row(h, heads, False))
        delta = jnp.sum(prod * own, axis=1, keepdims=True)
        for i, part in enumerate(split3(-delta)):
            ext = ext + part * lanes(256, lambda l: l == hw + 1 + 3 * h + i)
    do_ext = ext.astype(BF)
    kt = k.T
    at_mask = lanes(256, lambda l: l == hw)
    dk = jnp.zeros((rows, 256), F32)
    dv = jnp.zeros((rows, 256), F32)
    dqs = []
    for h in range(heads):
        row = lanes(256, head_row(h, heads, True))
        qh = q * (row + at_mask).astype(BF)
        doh = do_ext * row.astype(BF)
        p = jnp.exp(dot(k, qh, NT))
        ds = (p * dot(v, doh, NT)).astype(BF)
        dv = dv + dot(p.astype(BF), doh)
        dk = dk + dot(ds, qh)
        dqs.append(dot(kt[h * HD : (h + 1) * HD], ds))
    dqs.append(jnp.zeros((256 - hw, rows), F32))
    dq = jnp.concatenate(dqs, 0).T * 0.125
    real = lanes(256, lambda l: l < hw)
    return dq.astype(BF), (dk * real).astype(BF), (dv * real).astype(BF)


def over_pairs(b, refs, dst, *, nshort, short_slot, heads, blk):
    sub = blk // short_slot
    long0 = nshort // sub

    def one(row, rows):
        sl = pl.ds(row, rows)
        for c, val in enumerate(attn_bwd_pair(refs, sl, rows, heads)):
            dst(sl, c, val)

    @pl.when(b < long0)
    def _():
        for i in range(sub):
            one(i * short_slot, short_slot)

    @pl.when(b >= long0)
    def _():
        one(0, blk)


def bwd_own_kernel(xs_ref, xl_ref, p_ref, o_ref, do_ref, dp_ref, gw_ref, gb_ref, **kw):
    b = pl.program_id(0)
    long0 = kw["nshort"] * kw["short_slot"] // kw["blk"]

    def dst(sl, c, val):
        dp_ref[sl, 256 * c : 256 * (c + 1)] = val

    over_pairs(b, (p_ref, o_ref, do_ref), dst, **kw)

    @pl.when(b == 0)
    def _():
        gw_ref[...] = jnp.zeros_like(gw_ref)
        gb_ref[...] = jnp.zeros_like(gb_ref)

    @pl.when(b < long0)
    def _():
        gw_ref[...] += dot(xs_ref[...], dp_ref[...], TN)

    @pl.when(b >= long0)
    def _():
        gw_ref[...] += dot(xl_ref[...], dp_ref[...], TN)

    gb_ref[...] += jnp.sum(dp_ref[...].astype(F32).reshape(-1, 8, 768), axis=0)


def bwd_own(xs, xl, p, o, do, blk, **kw):
    rows, d = xs.shape[0] + xl.shape[0], xs.shape[1]
    return pl.pallas_call(
        lambda *r: bwd_own_kernel(*r, blk=blk, **kw),
        grid=(rows // blk,),
        in_specs=blocks(blk, d, xs.shape[0] // blk)
        + [
            pl.BlockSpec((1, blk, 768), lambda b: (0, b, 0)),
            pl.BlockSpec((1, blk, 256), lambda b: (0, b, 0)),
            pl.BlockSpec((1, blk, 256), lambda b: (0, b, 0)),
        ],
        out_specs=[
            pl.BlockSpec((blk, 768), lambda b: (b, 0)),
            pl.BlockSpec((d, 768), lambda b: (0, 0)),
            pl.BlockSpec((8, 768), lambda b: (0, 0)),
        ],
        out_shape=[
            jax.ShapeDtypeStruct((rows, 768), BF),
            jax.ShapeDtypeStruct((d, 768), F32),
            jax.ShapeDtypeStruct((8, 768), F32),
        ],
        compiler_params=pltpu.CompilerParams(vmem_limit_bytes=60 * 2**20),
        cost_estimate=pl.CostEstimate(flops=18 * 10**9, bytes_accessed=2**23, transcendentals=0),
        name="attn_bwd_own",
    )(xs, xl, p, o, do)


def bwd_rest_kernel(
    place_ref, p_ref, o_ref, do_ref, own_ref, dh_ref, w_hbm, *refs, lo, **kw
):
    pieces, gs_ref, (gl_ref, dp_s, w_s, stage, sems, sem) = refs[:8], refs[8], refs[-6:]
    b, g = pl.program_id(0) + lo, pl.program_id(1)
    slots = w_s.shape[0]
    hw = kw["heads"] * HD
    long0 = kw["nshort"] * kw["short_slot"] // kw["blk"]

    @pl.when((b == lo) & (g == 0))
    def _():
        own = [
            pltpu.make_async_copy(
                w_hbm.at[pl.ds(c * hw, hw)], w_s.at[0, pl.ds(256 * c, hw)], sem.at[c]
            )
            for c in range(3)
        ]
        w_s[...] = jnp.zeros_like(w_s)
        for c in own:
            c.start()

        def store(n):
            def put(at):
                row = place_ref[1, n]

                @pl.when(row >= 0)
                def _():
                    @pl.loop(0, slots - 1)
                    def _(j):
                        w_s[j + 1, pl.ds(pl.multiple_of(row, 32), stage.shape[2])] = stage[
                            at, j
                        ].astype(BF)

            return put

        fetch([(pieces[n], None, store(n)) for n in range(8)], stage, sems, 3)
        for c in own:
            c.wait()

    @pl.when(g == 0)
    def _():
        dp_s[0] = own_ref[...]

    def dst(sl, c, val):
        dp_s[g + 1, sl, 256 * c : 256 * (c + 1)] = val

    over_pairs(b, (p_ref, o_ref, do_ref), dst, **kw)

    @pl.when(g == slots - 2)
    def _():
        acc = dh_ref[...]
        for j in range(slots):
            acc = acc + dot(dp_s[j], w_s[j])

        if lo < long0:

            @pl.when(b < long0)
            def _():
                gs_ref[...] = acc

        @pl.when(b >= long0)
        def _():
            gl_ref[...] = acc


def bwd_rest(lo, hi, prev, place, p, o, do, own_dp, dh, w_own, pieces, srows, blk, **kw):
    slots, rows, _ = p.shape
    d = dh.shape[1]
    r = pieces[0].shape[1]

    long0 = srows // blk
    assert lo == 0 or lo >= long0
    last = lo > 0

    def grp_map(b, g, *_):
        return (g + 1, b + lo, 0)

    return pl.pallas_call(
        lambda *r: bwd_rest_kernel(*r, lo=lo, blk=blk, **kw),
        grid_spec=pltpu.PrefetchScalarGridSpec(
            num_scalar_prefetch=1,
            grid=(hi - lo, slots - 1),
            in_specs=[
                pl.BlockSpec((1, blk, 768), grp_map),
                pl.BlockSpec((1, blk, 256), grp_map),
                pl.BlockSpec((1, blk, 256), grp_map),
                pl.BlockSpec((blk, 768), lambda b, g, *_: (b + lo, 0)),
                pl.BlockSpec((blk, d), lambda b, g, *_: (b + lo, 0)),
            ]
            + [pl.BlockSpec(memory_space=pl.ANY)] * (9 + last),
            out_specs=[pl.BlockSpec((blk, d), lambda b, g, *_: (b + lo - long0, 0))]
            if last
            else blocks(blk, d, long0),
            scratch_shapes=[
                pltpu.VMEM((slots, blk, 768), BF),
                pltpu.VMEM((slots, 768, d), BF),
                pltpu.VMEM((3, slots - 1, r, d), F32),
                pltpu.SemaphoreType.DMA((3,)),
                pltpu.SemaphoreType.DMA((3,)),
            ],
        ),
        out_shape=[
            jax.ShapeDtypeStruct((srows, d), F32),
            jax.ShapeDtypeStruct((rows - srows, d), F32),
        ][last:],
        input_output_aliases={15: 0} if last else {},
        compiler_params=pltpu.CompilerParams(vmem_limit_bytes=60 * 2**20),
        cost_estimate=pl.CostEstimate(flops=25 * 10**9, bytes_accessed=2**23, transcendentals=0),
        name="attn_bwd_rest",
    )(place, p, o, do, own_dp, dh, w_own, *pieces, *([prev] if last else []))


def norm_stats(h):
    center = h - jnp.mean(h, -1, keepdims=True)
    rstd = lax.rsqrt(jnp.mean(center * center, -1, keepdims=True) + EPS)
    return center * rstd, rstd


def norm_back(dy, xhat, rstd, gain):
    s = dy * gain
    return rstd * (
        s - jnp.mean(s, -1, keepdims=True) - xhat * jnp.mean(s * xhat, -1, keepdims=True)
    )


def gelu_both(u):
    phi = 0.5 + 0.5 * lax.erf(u * 0.7071067811865476)
    pdf = jnp.exp2(u * u * (-0.5 * 1.4426950408889634)) * 0.3989422804014327
    return u * phi, phi + u * pdf


def row8(x):
    return jnp.sum(x.reshape(-1, 8, x.shape[-1]), axis=0)


def ffn_kernel(place_ref, *refs, long0, hw):
    (xs_ref, xl_ref, cs_ref, cl_ref, o_ref, vec_ref, bup_ref, w1_hbm, wu_hbm, wd_hbm) = refs[:10]
    w1_pieces, w2_pieces = refs[10:18], refs[18:26]
    (es_ref, el_ref, dh_ref, do_ref, gall_ref) = refs[26:31]
    (wo_s, wu_s, wd_s, stage, sems, sem, g_s, gp_s, du_s, sm_s, x_s, c_s) = refs[31:]
    i = pl.program_id(0)
    slots, d, fl = wu_s.shape
    r = stage.shape[2]

    @pl.when(i == 0)
    def _():
        wo_s[...] = jnp.zeros_like(wo_s)
        own = [
            pltpu.make_async_copy(wu_hbm, wu_s.at[0], sem.at[0]),
            pltpu.make_async_copy(wd_hbm, wd_s.at[0], sem.at[1]),
            pltpu.make_async_copy(
                w1_hbm.at[pl.ds(3 * hw, hw)], wo_s.at[0, pl.ds(0, hw)], sem.at[2]
            ),
        ]
        for c in own:
            c.start()

        def store(dst, n):
            def put(at):
                row = pl.multiple_of(place_ref[0, n], 32)

                @pl.loop(0, slots - 1)
                def _(j):
                    dst[j + 1, pl.ds(row, r)] = stage[at, j].astype(BF)

            return put

        def store_out(n):
            def put(at):
                row = place_ref[2, n]

                @pl.when(row >= 0)
                def _():
                    @pl.loop(0, slots - 1)
                    def _(j):
                        wo_s[j + 1, pl.ds(pl.multiple_of(row, 32), r)] = stage[at, j].astype(BF)

            return put

        jobs = [(w1_pieces[n], None, store_out(n)) for n in range(8)]
        for n in range(8):
            jobs.append((w2_pieces[n].at[:, pl.ds(0, r)], None, store(wu_s, n)))
            jobs.append((w2_pieces[n].at[:, pl.ds(r, r)], None, store(wd_s, n)))
        fetch(jobs, stage, sems, 4)
        gall_ref[...] = jnp.zeros_like(gall_ref)
        sm_s[...] = jnp.zeros_like(sm_s)
        for c in own:
            c.wait()

    @pl.when(i < long0)
    def _():
        x_s[...] = xs_ref[...]
        c_s[...] = cs_ref[...]

    @pl.when(i >= long0)
    def _():
        x_s[...] = xl_ref[...]
        c_s[...] = cl_ref[...]

    def vec(n):
        return vec_ref[n : n + 1].astype(F32)

    attn = dot(o_ref[0], wo_s[0])
    for j in range(1, slots):
        attn = attn + dot(o_ref[j], wo_s[j])
    xhat1, rstd1 = norm_stats(x_s[...].astype(F32) + attn + vec(0))
    y1 = xhat1 * vec(2) + vec(4)
    y1b = y1.astype(BF)
    ffn = jnp.zeros_like(y1)
    for j in range(slots):
        u = dot(y1b, wu_s[j]) + bup_ref[j : j + 1]
        g, gp = gelu_both(u)
        gb = g.astype(BF)
        g_s[j] = gb
        gp_s[j] = gp
        ffn = ffn + dot(gb, wd_s[j])
    xhat2, rstd2 = norm_stats(y1 + ffn + vec(1))
    enc = (xhat2 * vec(3) + vec(5)).astype(BF)

    @pl.when(i < long0)
    def _():
        es_ref[...] = enc

    @pl.when(i >= long0)
    def _():
        el_ref[...] = enc

    dy = c_s[...].astype(F32)
    dh2 = norm_back(dy, xhat2, rstd2, vec(3))
    dz = dh2.astype(BF)
    sm_s[1] += row8(dh2)
    sm_s[3] += row8(dy * xhat2)
    sm_s[5] += row8(dy)
    dy1 = dh2
    for j in range(slots):
        du = (dot(dz, wd_s[j], NT) * gp_s[j]).astype(BF)
        du_s[j] = du
        dy1 = dy1 + dot(du, wu_s[j], NT)
    gall_ref[:, 0:fl] += dot(y1b, du_s[0], TN)
    gall_ref[:, fl : 2 * fl] += dot(dz, g_s[0], TN)
    sm_s[6] += row8(du_s[0].astype(F32))
    dh1 = norm_back(dy1, xhat1, rstd1, vec(2))
    dh_ref[...] = dh1
    da = dh1.astype(BF)
    sm_s[0] += row8(dh1)
    sm_s[2] += row8(dy1 * xhat1)
    sm_s[4] += row8(dy1)
    gall_ref[:, 2 * fl : 2 * fl + 256] += dot(da, o_ref[0], TN)
    for j in range(slots):
        do_ref[j] = dot(da, wo_s[j], NT).astype(BF)

    @pl.when(i == pl.num_programs(0) - 1)
    def _():
        small = jnp.sum(sm_s[...], axis=1)
        small = jnp.concatenate([small, jnp.zeros((120, d), F32)], 0)
        gall_ref[:, 2 * fl + 256 :] = small.T


def ffn_block(place, xs, xl, cs, cl, o, vecs, bup, own, pieces, hw, blk):
    srows, d = xs.shape
    rows = srows + xl.shape[0]
    slots = o.shape[0]
    fl = own[1].shape[1]
    r = pieces[0].shape[1]
    long0 = srows // blk
    row = lambda i, *_: (i, 0)
    grp = lambda i, *_: (0, i, 0)
    const = lambda i, *_: (0, 0)
    return pl.pallas_call(
        lambda *r: ffn_kernel(*r, long0=long0, hw=hw),
        grid_spec=pltpu.PrefetchScalarGridSpec(
            num_scalar_prefetch=1,
            grid=(rows // blk,),
            in_specs=blocks(blk, d, long0)
            + blocks(blk, d, long0)
            + [
                pl.BlockSpec((slots, blk, 256), grp),
                pl.BlockSpec((8, d), const),
                pl.BlockSpec((slots, fl), const),
            ]
            + [pl.BlockSpec(memory_space=pl.ANY)] * 19,
            out_specs=blocks(blk, d, long0)
            + [
                pl.BlockSpec((blk, d), row),
                pl.BlockSpec((slots, blk, 256), grp),
                pl.BlockSpec((d, 2 * fl + 384), const, pipeline_mode=pl.Buffered(1)),
            ],
            scratch_shapes=[
                pltpu.VMEM((slots, 256, d), BF),
                pltpu.VMEM((slots, d, fl), BF),
                pltpu.VMEM((slots, fl, d), BF),
                pltpu.VMEM((4, slots - 1, r, d), F32),
                pltpu.SemaphoreType.DMA((4,)),
                pltpu.SemaphoreType.DMA((3,)),
                pltpu.VMEM((slots, blk, fl), BF),
                pltpu.VMEM((slots, blk, fl), F32),
                pltpu.VMEM((slots, blk, fl), BF),
                pltpu.VMEM((8, 8, d), F32),
                pltpu.VMEM((blk, d), BF),
                pltpu.VMEM((blk, d), BF),
            ],
        ),
        out_shape=[
            jax.ShapeDtypeStruct((srows, d), BF),
            jax.ShapeDtypeStruct((rows - srows, d), BF),
            jax.ShapeDtypeStruct((rows, d), F32),
            jax.ShapeDtypeStruct((slots, rows, 256), BF),
            jax.ShapeDtypeStruct((d, 2 * fl + 384), F32),
        ],
        compiler_params=pltpu.CompilerParams(vmem_limit_bytes=62 * 2**20),
        cost_estimate=pl.CostEstimate(flops=80 * 10**9, bytes_accessed=2**25, transcendentals=0),
        name="ffn_block",
    )(place, xs, xl, cs, cl, o, vecs, bup, *own, *pieces)


class Wires:
    def __init__(self, n_dp, n_tensor):
        self.n_dp, self.n_tensor = n_dp, n_tensor
        self.first = [(i, i ^ (4 if i & 1 else 2)) for i in range(n_dp)]
        self.second = [(i, i ^ (2 if i & 1 else 4)) for i in range(n_dp)]
        self.pair = [(i, i ^ 1) for i in range(n_dp)]
        me = lax.axis_index("dp")
        odd = (me & 1).astype(jnp.int32)
        a, b = 2 + 2 * odd, 4 - 2 * odd
        masks = [0, a, b, 6, 1, 1 ^ b, 1 ^ a, 7]
        self.low = (me & 7).astype(jnp.int32)
        self.odd, self.x, self.y = odd, (self.low >> 1) & 1, self.low >> 2
        self.source = jnp.stack([jnp.asarray(self.low ^ m, jnp.int32) for m in masks])

    def piece(self, shard):
        extra = self.n_dp // 8
        r = shard.shape[0] // self.n_dp
        at = (self.low * extra + lax.axis_index("dp") // 8) * r
        return lax.dynamic_slice_in_dim(shard, at, r, 0).astype(F32)

    def along_tensor(self, piece):
        n = self.n_tensor
        return [
            lax.ppermute(piece, "tensor", [(i, (i + s) % n) for i in range(n)]) for s in range(1, n)
        ]

    def whole_eighth(self, z):
        if self.n_dp == 8:
            return z
        groups = [[g + 8 * e for e in range(self.n_dp // 8)] for g in range(8)]
        return lax.all_gather(z, "dp", axis=z.ndim - 2, tiled=True, axis_index_groups=groups)

    def first_hop(self, z):
        return lax.ppermute(z, "dp", self.first), lax.ppermute(z, "dp", self.second)

    def second_hop(self, a):
        return lax.ppermute(a, "dp", self.second)

    def to_pair(self, x):
        return lax.ppermute(x, "dp", self.pair)


    def split(self, g):
        rows, width = g.shape
        return g.reshape(self.n_dp // 8, 4, 2, rows // self.n_dp, width)

    def halve_pair(self, g):
        return self.to_pair(lax.dynamic_index_in_dim(g, 1 - self.odd, 2, keepdims=False))

    def sum_pair(self, g, got):
        return lax.dynamic_index_in_dim(g, self.odd, 2, keepdims=False) + got

    def two(self, h, x, y):
        n = jnp.where(self.odd == 1, 2 * y, x)
        m = jnp.where(self.odd == 1, 2 * y + 1, x + 2)
        return jnp.concatenate([lax.dynamic_slice_in_dim(h, i, 1, 1) for i in (n, m)], 1)

    def halve_first(self, h):
        return lax.ppermute(self.two(h, 1 - self.x, 1 - self.y), "dp", self.first)

    def sum_first(self, h, got):
        return self.two(h, self.x, self.y) + got

    def halve_second(self, k):
        at = jnp.where(self.odd == 1, self.x, self.y)
        return lax.ppermute(lax.dynamic_index_in_dim(k, 1 - at, 1, keepdims=False), "dp", self.second)

    def sum_second(self, k, got):
        at = jnp.where(self.odd == 1, self.x, self.y)
        out = lax.dynamic_index_in_dim(k, at, 1, keepdims=False) + got
        if self.n_dp == 8:
            return out[0]
        groups = [[g + 8 * e for e in range(self.n_dp // 8)] for g in range(8)]
        return lax.psum_scatter(out, "dp", scatter_dimension=0, axis_index_groups=groups)


def after(x, *others):
    return lax.optimization_barrier((x, *others))[0]


def make(n_dp, n_tensor):
    def on_device(
        short_tokens,
        short_lengths,
        long_tokens,
        long_lengths,
        w_qkv,
        b_qv,
        w_out,
        res_biases,
        ln_gains,
        ln_shifts,
        w_up,
        b_up,
        w_down,
        short_cotangent,
        long_cotangent,
    ):
        ns, ss, d = short_tokens.shape
        nl, ls, _ = long_tokens.shape
        srows = ns * ss
        heads, hd = b_qv.shape[1], b_qv.shape[2]
        hw = heads * hd
        blk = ls
        kw = dict(nshort=ns, short_slot=ss, heads=heads, blk=blk)
        wires = Wires(n_dp, n_tensor)
        r = w_up.shape[0] // 8

        w1_own = jnp.concatenate([w_qkv.transpose(0, 2, 1).reshape(3 * hw, d), w_out], 0)
        tail = jnp.zeros((d - 2 * hw,), F32)
        small = jnp.stack([b_up[0].astype(F32), jnp.concatenate([b_qv.reshape(2 * hw).astype(F32), tail])])
        small = jnp.concatenate([small, jnp.zeros((6, d), F32)], 0)
        piece = wires.piece(w1_own)
        pr = piece.shape[0]
        z = wires.along_tensor(jnp.concatenate([small, piece], 0))
        row = wires.source * r
        c = row // hw
        place = jnp.stack(
            [row, jnp.where(c < 3, c * 256 + row - c * hw, -1), jnp.where(c < 3, -1, row - 3 * hw)]
        )

        one = np.zeros((256 - hw,), np.float32)
        one[1 : 1 + 3 * heads] = 1.0
        one = jnp.asarray(one)

        def bias_of(sm):
            zero = jnp.zeros((256 - hw,), F32)
            none = jnp.zeros((hw,), F32)
            return jnp.concatenate([sm[1, :hw], zero, none, one, sm[1, hw : 2 * hw], one])[None]

        xs, xl = short_tokens.reshape(srows, d), long_tokens.reshape(-1, d)
        cs, cl = short_cotangent.reshape(srows, d), long_cotangent.reshape(-1, d)
        lens = jnp.concatenate([short_lengths, long_lengths])
        po = attn_fwd(0, lens, place, xs, xl, w1_own, bias_of(small), None, slots=n_tensor, **kw)

        t1 = wires.whole_eighth(after(jnp.stack([x[8:] for x in z]), po[1]))
        a1, b1 = wires.first_hop(t1)
        piece2 = after(jnp.stack([wires.piece(w_up), wires.piece(w_down)]), po[1])
        z2 = wires.along_tensor(piece2)
        c1 = wires.second_hop(after(a1, z2[0]))
        w1 = [t1, a1, b1, c1]
        w1 += [wires.to_pair(x) for x in w1[:3]] + [wires.to_pair(after(c1, z2[2]))]
        for s in range(1, n_tensor):
            po = attn_fwd(s, lens, place, xs, xl, w1, bias_of(z[s - 1]), po, slots=n_tensor, **kw)
            if s == 1:
                *z2, p, o = lax.optimization_barrier((*z2, *po))
                po = p, o
                t2 = wires.whole_eighth(jnp.stack(z2))
                t2 = t2.reshape(n_tensor - 1, -1, d)
                a2, b2 = wires.first_hop(t2)
        t2, a2, b2, *po = lax.optimization_barrier((t2, a2, b2, *po))
        w2 = [t2, a2, b2, wires.second_hop(a2)]
        w2 += [wires.to_pair(x) for x in w2]
        p, o = po
        bup = jnp.stack([x[0] for x in [small] + z])
        vecs = jnp.concatenate([res_biases, ln_gains, ln_shifts, jnp.zeros((2, d), BF)], 0).astype(F32)
        es, el, dh, do, gall = ffn_block(
            place, xs, xl, cs, cl, o, vecs, bup, [w1_own, w_up, w_down], w1 + w2, hw, 256
        )
        fl = w_up.shape[1]
        gall = wires.split(gall)
        got = wires.halve_pair(gall)
        dp_own, gw, gb = bwd_own(xs, xl, p, o, do, **kw)
        gall = wires.sum_pair(gall, after(got, dp_own))
        got = wires.halve_first(gall)
        gb = gb.sum(0).reshape(3, 256)
        gb = jnp.stack([gb[0, :hw], gb[2, :hw]]).reshape(2 * heads, n_dp, hd // n_dp)
        gb = gb.transpose(1, 0, 2).reshape(n_dp, 1, -1)
        gw = lax.dynamic_update_slice(gw.reshape(n_dp, d // n_dp, 768), gb, (0, 0, hw))
        gw = wires.split(gw.reshape(d, 768))
        gotw = wires.halve_pair(gw)
        nb = (ns * ss + nl * ls) // blk
        rest = (place, p, o, do, dp_own, dh, w1_own, w1, srows)
        gs, gl = bwd_rest(0, nb // 2, None, *rest, **kw)
        got, gotw, gl = lax.optimization_barrier((got, gotw, gl))
        gall = wires.sum_first(gall, got)
        got = wires.halve_second(gall)
        gw = wires.sum_pair(gw, gotw)
        gotw = wires.halve_first(gw)
        (gl,) = bwd_rest(nb // 2, nb, gl, *rest, **kw)
        got, gotw, gl = lax.optimization_barrier((got, gotw, gl))
        gw = wires.sum_first(gw, gotw)
        gotw = wires.halve_second(gw)
        gall = wires.sum_second(gall, got)
        gw = wires.sum_second(gw, gotw)
        small_shard = gall[:, 2 * fl + 256 : 2 * fl + 264].T
        gqkv = gw.reshape(-1, 3, 256)[:, :, :hw].transpose(1, 0, 2)
        qv_shard = gw[0, hw : hw + 2 * hw // n_dp].reshape(2, heads, hd // n_dp)
        return (
            es.reshape(ns, ss, d),
            el.reshape(nl, ls, d),
            gs.reshape(ns, ss, d),
            gl.reshape(nl, ls, d),
            gqkv,
            qv_shard,
            gall[:, 2 * fl : 2 * fl + hw].T,
            small_shard[0:2],
            small_shard[2:4],
            small_shard[4:6],
            gall[:, :fl],
            small_shard[6:7],
            gall[:, fl : 2 * fl].T,
        )

    return on_device


def solution(mesh):
    tok = P("dp", None, None)
    return jax.shard_map(
        make(mesh.shape["dp"], mesh.shape["tensor"]),
        mesh=mesh,
        in_specs=(
            tok,
            P("dp"),
            tok,
            P("dp"),
            P(None, None, "tensor"),
            P(None, "tensor", None),
            P("tensor", None),
            P(),
            P(),
            P(),
            P(None, "tensor"),
            P("tensor", None),
            P("tensor", None),
            tok,
            tok,
        ),
        out_specs=(
            tok,
            tok,
            tok,
            tok,
            P(None, "dp", "tensor"),
            P(None, "tensor", "dp"),
            P("tensor", "dp"),
            P(None, "dp"),
            P(None, "dp"),
            P(None, "dp"),
            P("dp", "tensor"),
            P("tensor", "dp"),
            P("tensor", "dp"),
        ),
        check_vma=False,
    )
```

```python
import jax
import jax.numpy as jnp
import numpy as np
from jax import lax
from jax.experimental import pallas as pl
from jax.experimental.pallas import tpu as pltpu
from jax.sharding import PartitionSpec as P

HD = 64
EPS = 1e-12
BF = jnp.bfloat16
F32 = jnp.float32
NT = (((1,), (1,)), ((), ()))
TN = (((0,), (0,)), ((), ()))


def dot(a, b, dims=(((1,), (0,)), ((), ()))):
    return lax.dot_general(a, b, dims, preferred_element_type=F32)


def lanes(width, test):
    lane = lax.broadcasted_iota(jnp.int32, (1, width), 1)
    return jnp.where(test(lane), 1.0, 0.0).astype(F32)


def head_row(h, width, extra):
    w = width * HD

    def test(lane):
        own = (lane >= h * HD) & (lane < (h + 1) * HD)
        if extra:
            own = own | ((lane >= w + 1 + 3 * h) & (lane < w + 4 + 3 * h))
        return own

    return test


def split3(x):
    hi = x.astype(BF).astype(F32)
    rest = x - hi
    mid = rest.astype(BF).astype(F32)
    return hi, mid, rest - mid


def blocks(blk, d, nshort, grid_pos=0):
    return [
        pl.BlockSpec((blk, d), lambda *g: (jnp.minimum(g[grid_pos], nshort - 1), 0)),
        pl.BlockSpec((blk, d), lambda *g: (jnp.maximum(g[grid_pos] - nshort, 0), 0)),
    ]


def fetch(jobs, stage, sems, depth):
    def copy(n):
        src, idx, _ = jobs[n]
        dst = stage.at[n % depth] if idx is None else stage.at[n % depth, idx]
        return pltpu.make_async_copy(src, dst, sems.at[n % depth])

    for n in range(min(depth - 1, len(jobs))):
        copy(n).start()
    for n in range(len(jobs)):
        if n + depth - 1 < len(jobs):
            copy(n + depth - 1).start()
        copy(n).wait()
        jobs[n][2](n % depth)


def attn_fwd_kernel(
    len_ref, place_ref, slot_ref, xs_ref, xl_ref, b_ref, *refs, own, nshort, short_slot, heads, blk
):
    if not own:
        pieces, (p_ref, o_ref, w_s, x_s, stage, sems) = refs[:8], refs[-6:]
    else:
        w_ref, p_ref, o_ref, w_s, x_s = refs
    hw = heads * HD
    b = pl.program_id(0)
    sub = blk // short_slot
    long0 = nshort // sub

    @pl.when(b == 0)
    def _():
        if not own:
            at = slot_ref[0] - 1
            copies = [
                pltpu.make_async_copy(pieces[n].at[at], stage.at[n], sems.at[n])
                for n in range(8)
            ]
            for c in copies:
                c.start()
            w_s[...] = jnp.zeros_like(w_s)
            r = stage.shape[1]
            for n in range(8):
                copies[n].wait()
                row = place_ref[1, n]

                @pl.when(row >= 0)
                def _():
                    w_s[pl.ds(pl.multiple_of(row, 32), r)] = stage[n].astype(BF)

        else:
            w_s[...] = jnp.zeros_like(w_s)
            for c in range(3):
                w_s[256 * c : 256 * c + hw] = w_ref[c * hw : (c + 1) * hw]

    @pl.when(b < long0)
    def _():
        x_s[...] = xs_ref[...]

    @pl.when(b >= long0)
    def _():
        x_s[...] = xl_ref[...]

    p_ref[0] = (dot(x_s[...], w_s[...], NT) + b_ref[...]).astype(BF)

    def pair(row, rows, length):
        sl = pl.ds(row, rows)
        pos = lax.broadcasted_iota(jnp.int32, (rows, 1), 0)
        hidden = jnp.where(pos < length, 0.0, -1e30)
        at_mask = lanes(256, lambda l: l == hw)
        q = (p_ref[0, sl, 0:256].astype(F32) * 0.125 + at_mask).astype(BF)
        k = (p_ref[0, sl, 256:512].astype(F32) + hidden * at_mask).astype(BF)
        v = p_ref[0, sl, 512:768]
        p_ref[0, sl, 256:512] = k
        out = jnp.zeros((rows, 256), F32)
        ext = jnp.zeros((rows, 256), F32)
        for h in range(heads):
            own = lanes(256, head_row(h, heads, False))
            s = dot(q * (own + at_mask).astype(BF), k, NT)
            m = jnp.max(s, axis=1, keepdims=True)
            e = jnp.exp(s - m)
            total = jnp.sum(e, axis=1, keepdims=True)
            a = (e * (1.0 / total)).astype(BF)
            out = out + dot(a, v * own.astype(BF))
            for i, part in enumerate(split3(-(m + jnp.log(total)))):
                ext = ext + part * lanes(256, lambda l: l == hw + 1 + 3 * h + i)
        p_ref[0, sl, 0:256] = (q.astype(F32) + ext).astype(BF)
        o_ref[0, sl] = out.astype(BF)

    @pl.when(b < long0)
    def _():
        @pl.loop(0, sub)
        def _(i):
            pair(pl.multiple_of(i * short_slot, short_slot), short_slot, len_ref[b * sub + i])

    @pl.when(b >= long0)
    def _():
        pair(0, blk, len_ref[nshort + b - long0])


def attn_fwd(slot, lens, place, xs, xl, w, bias, prev, nshort, short_slot, heads, blk, slots):
    rows, d = xs.shape[0] + xl.shape[0], xs.shape[1]
    in_specs = blocks(blk, d, xs.shape[0] // blk) + [pl.BlockSpec((1, 768), lambda b, *_: (0, 0))]
    args = [xs, xl, bias]
    scratch = [pltpu.VMEM((768, d), BF), pltpu.VMEM((blk, d), BF)]
    aliases = {}
    if slot:
        in_specs += [pl.BlockSpec(memory_space=pl.ANY)] * 10
        args += list(w) + list(prev)
        aliases = {14: 0, 15: 1}
        r = w[0].shape[1]
        scratch += [pltpu.VMEM((8, r, d), F32), pltpu.SemaphoreType.DMA((8,))]
    else:
        in_specs.append(pl.BlockSpec(w.shape, lambda b, *_: (0, 0)))
        args.append(w)
    return pl.pallas_call(
        lambda *r: attn_fwd_kernel(
            *r, own=slot == 0, nshort=nshort, short_slot=short_slot, heads=heads, blk=blk
        ),
        grid_spec=pltpu.PrefetchScalarGridSpec(
            num_scalar_prefetch=3,
            grid=(rows // blk,),
            in_specs=in_specs,
            out_specs=[
                pl.BlockSpec((1, blk, 768), lambda b, ln, at, sl: (sl[0], b, 0)),
                pl.BlockSpec((1, blk, 256), lambda b, ln, at, sl: (sl[0], b, 0)),
            ],
            scratch_shapes=scratch,
        ),
        out_shape=[
            jax.ShapeDtypeStruct((slots, rows, 768), BF),
            jax.ShapeDtypeStruct((slots, rows, 256), BF),
        ],
        input_output_aliases=aliases,
        compiler_params=pltpu.CompilerParams(vmem_limit_bytes=60 * 2**20),
        cost_estimate=pl.CostEstimate(flops=14 * 10**9, bytes_accessed=2**23, transcendentals=0),
        name="attn_fwd",
    )(lens, place, jnp.full((1,), slot, jnp.int32), *args)


def attn_bwd_pair(refs, sl, rows, heads):
    p_ref, o_ref, do_ref = refs
    hw = heads * HD
    q, k, v = p_ref[0, sl, 0:256], p_ref[0, sl, 256:512], p_ref[0, sl, 512:768]
    do = do_ref[0, sl]
    do32 = do.astype(F32)
    prod = do32 * o_ref[0, sl].astype(F32)
    ext = do32
    for h in range(heads):
        own = lanes(256, head_row(h, heads, False))
        delta = jnp.sum(prod * own, axis=1, keepdims=True)
        for i, part in enumerate(split3(-delta)):
            ext = ext + part * lanes(256, lambda l: l == hw + 1 + 3 * h + i)
    do_ext = ext.astype(BF)
    kt = k.T
    at_mask = lanes(256, lambda l: l == hw)
    dk = jnp.zeros((rows, 256), F32)
    dv = jnp.zeros((rows, 256), F32)
    dqs = []
    for h in range(heads):
        row = lanes(256, head_row(h, heads, True))
        qh = q * (row + at_mask).astype(BF)
        doh = do_ext * row.astype(BF)
        p = jnp.exp(dot(k, qh, NT))
        ds = (p * dot(v, doh, NT)).astype(BF)
        dv = dv + dot(p.astype(BF), doh)
        dk = dk + dot(ds, qh)
        dqs.append(dot(kt[h * HD : (h + 1) * HD], ds))
    dqs.append(jnp.zeros((256 - hw, rows), F32))
    dq = jnp.concatenate(dqs, 0).T * 0.125
    real = lanes(256, lambda l: l < hw)
    return dq.astype(BF), (dk * real).astype(BF), (dv * real).astype(BF)


def over_pairs(b, refs, dst, *, nshort, short_slot, heads, blk):
    sub = blk // short_slot
    long0 = nshort // sub

    def one(row, rows):
        sl = pl.ds(row, rows)
        for c, val in enumerate(attn_bwd_pair(refs, sl, rows, heads)):
            dst(sl, c, val)

    @pl.when(b < long0)
    def _():
        @pl.loop(0, sub)
        def _(i):
            one(pl.multiple_of(i * short_slot, short_slot), short_slot)

    @pl.when(b >= long0)
    def _():
        one(0, blk)


def bwd_own_kernel(xs_ref, xl_ref, p_ref, o_ref, do_ref, dp_ref, gw_ref, gb_ref, **kw):
    b = pl.program_id(0)
    long0 = kw["nshort"] * kw["short_slot"] // kw["blk"]

    def dst(sl, c, val):
        dp_ref[sl, 256 * c : 256 * (c + 1)] = val

    over_pairs(b, (p_ref, o_ref, do_ref), dst, **kw)

    @pl.when(b == 0)
    def _():
        gw_ref[...] = jnp.zeros_like(gw_ref)
        gb_ref[...] = jnp.zeros_like(gb_ref)

    @pl.when(b < long0)
    def _():
        gw_ref[...] += dot(xs_ref[...], dp_ref[...], TN)

    @pl.when(b >= long0)
    def _():
        gw_ref[...] += dot(xl_ref[...], dp_ref[...], TN)

    gb_ref[...] += jnp.sum(dp_ref[...].astype(F32).reshape(-1, 8, 768), axis=0)


def bwd_own(xs, xl, p, o, do, blk, **kw):
    rows, d = xs.shape[0] + xl.shape[0], xs.shape[1]
    return pl.pallas_call(
        lambda *r: bwd_own_kernel(*r, blk=blk, **kw),
        grid=(rows // blk,),
        in_specs=blocks(blk, d, xs.shape[0] // blk)
        + [
            pl.BlockSpec((1, blk, 768), lambda b: (0, b, 0)),
            pl.BlockSpec((1, blk, 256), lambda b: (0, b, 0)),
            pl.BlockSpec((1, blk, 256), lambda b: (0, b, 0)),
        ],
        out_specs=[
            pl.BlockSpec((blk, 768), lambda b: (b, 0)),
            pl.BlockSpec((d, 768), lambda b: (0, 0)),
            pl.BlockSpec((8, 768), lambda b: (0, 0)),
        ],
        out_shape=[
            jax.ShapeDtypeStruct((rows, 768), BF),
            jax.ShapeDtypeStruct((d, 768), F32),
            jax.ShapeDtypeStruct((8, 768), F32),
        ],
        compiler_params=pltpu.CompilerParams(vmem_limit_bytes=60 * 2**20),
        cost_estimate=pl.CostEstimate(flops=18 * 10**9, bytes_accessed=2**23, transcendentals=0),
        name="attn_bwd_own",
    )(xs, xl, p, o, do)


def bwd_rest_kernel(
    place_ref, p_ref, o_ref, do_ref, own_ref, dh_ref, w_hbm, *refs, lo, **kw
):
    pieces, gs_ref, (gl_ref, dp_s, w_s, stage, sems, sem) = refs[:8], refs[8], refs[-6:]
    b, g = pl.program_id(0) + lo, pl.program_id(1)
    slots = w_s.shape[0]
    hw = kw["heads"] * HD
    long0 = kw["nshort"] * kw["short_slot"] // kw["blk"]

    @pl.when((b == lo) & (g == 0))
    def _():
        own = [
            pltpu.make_async_copy(
                w_hbm.at[pl.ds(c * hw, hw)], w_s.at[0, pl.ds(256 * c, hw)], sem.at[c]
            )
            for c in range(3)
        ]
        w_s[...] = jnp.zeros_like(w_s)
        for c in own:
            c.start()

        def store(n):
            def put(at):
                row = place_ref[1, n]

                @pl.when(row >= 0)
                def _():
                    @pl.loop(0, slots - 1)
                    def _(j):
                        w_s[j + 1, pl.ds(pl.multiple_of(row, 32), stage.shape[2])] = stage[
                            at, j
                        ].astype(BF)

            return put

        fetch([(pieces[n], None, store(n)) for n in range(8)], stage, sems, 3)
        for c in own:
            c.wait()

    @pl.when(g == 0)
    def _():
        dp_s[0] = own_ref[...]

    def dst(sl, c, val):
        dp_s[g + 1, sl, 256 * c : 256 * (c + 1)] = val

    over_pairs(b, (p_ref, o_ref, do_ref), dst, **kw)

    @pl.when(g == slots - 2)
    def _():
        acc = dh_ref[...]
        for j in range(slots):
            acc = acc + dot(dp_s[j], w_s[j])

        if lo < long0:

            @pl.when(b < long0)
            def _():
                gs_ref[...] = acc

        @pl.when(b >= long0)
        def _():
            gl_ref[...] = acc


def bwd_rest(lo, hi, prev, place, p, o, do, own_dp, dh, w_own, pieces, srows, blk, **kw):
    slots, rows, _ = p.shape
    d = dh.shape[1]
    r = pieces[0].shape[1]

    long0 = srows // blk
    assert lo == 0 or lo >= long0
    last = lo > 0

    def grp_map(b, g, *_):
        return (g + 1, b + lo, 0)

    return pl.pallas_call(
        lambda *r: bwd_rest_kernel(*r, lo=lo, blk=blk, **kw),
        grid_spec=pltpu.PrefetchScalarGridSpec(
            num_scalar_prefetch=1,
            grid=(hi - lo, slots - 1),
            in_specs=[
                pl.BlockSpec((1, blk, 768), grp_map),
                pl.BlockSpec((1, blk, 256), grp_map),
                pl.BlockSpec((1, blk, 256), grp_map),
                pl.BlockSpec((blk, 768), lambda b, g, *_: (b + lo, 0)),
                pl.BlockSpec((blk, d), lambda b, g, *_: (b + lo, 0)),
            ]
            + [pl.BlockSpec(memory_space=pl.ANY)] * (9 + last),
            out_specs=[pl.BlockSpec((blk, d), lambda b, g, *_: (b + lo - long0, 0))]
            if last
            else blocks(blk, d, long0),
            scratch_shapes=[
                pltpu.VMEM((slots, blk, 768), BF),
                pltpu.VMEM((slots, 768, d), BF),
                pltpu.VMEM((3, slots - 1, r, d), F32),
                pltpu.SemaphoreType.DMA((3,)),
                pltpu.SemaphoreType.DMA((3,)),
            ],
        ),
        out_shape=[
            jax.ShapeDtypeStruct((srows, d), F32),
            jax.ShapeDtypeStruct((rows - srows, d), F32),
        ][last:],
        input_output_aliases={15: 0} if last else {},
        compiler_params=pltpu.CompilerParams(vmem_limit_bytes=60 * 2**20),
        cost_estimate=pl.CostEstimate(flops=25 * 10**9, bytes_accessed=2**23, transcendentals=0),
        name="attn_bwd_rest",
    )(place, p, o, do, own_dp, dh, w_own, *pieces, *([prev] if last else []))


def norm_stats(h):
    center = h - jnp.mean(h, -1, keepdims=True)
    rstd = lax.rsqrt(jnp.mean(center * center, -1, keepdims=True) + EPS)
    return center * rstd, rstd


def norm_back(dy, xhat, rstd, gain):
    s = dy * gain
    return rstd * (
        s - jnp.mean(s, -1, keepdims=True) - xhat * jnp.mean(s * xhat, -1, keepdims=True)
    )


def gelu_both(u):
    phi = 0.5 + 0.5 * lax.erf(u * 0.7071067811865476)
    pdf = jnp.exp2(u * u * (-0.5 * 1.4426950408889634)) * 0.3989422804014327
    return u * phi, phi + u * pdf


def row8(x):
    return jnp.sum(x.reshape(-1, 8, x.shape[-1]), axis=0)


def ffn_kernel(place_ref, *refs, long0, hw):
    (xs_ref, xl_ref, cs_ref, cl_ref, o_ref, vec_ref, bup_ref, w1_hbm, wu_hbm, wd_hbm) = refs[:10]
    w1_pieces, w2_pieces = refs[10:18], refs[18:26]
    (es_ref, el_ref, dh_ref, do_ref, gall_ref) = refs[26:31]
    (wo_s, wu_s, wd_s, stage, sems, sem, g_s, gp_s, du_s, sm_s, x_s, c_s) = refs[31:]
    i = pl.program_id(0)
    slots, d, fl = wu_s.shape
    r = stage.shape[2]

    @pl.when(i == 0)
    def _():
        wo_s[...] = jnp.zeros_like(wo_s)
        own = [
            pltpu.make_async_copy(wu_hbm, wu_s.at[0], sem.at[0]),
            pltpu.make_async_copy(wd_hbm, wd_s.at[0], sem.at[1]),
            pltpu.make_async_copy(
                w1_hbm.at[pl.ds(3 * hw, hw)], wo_s.at[0, pl.ds(0, hw)], sem.at[2]
            ),
        ]
        for c in own:
            c.start()

        def store(dst, n):
            def put(at):
                row = pl.multiple_of(place_ref[0, n], 32)

                @pl.loop(0, slots - 1)
                def _(j):
                    dst[j + 1, pl.ds(row, r)] = stage[at, j].astype(BF)

            return put

        def store_out(n):
            def put(at):
                row = place_ref[2, n]

                @pl.when(row >= 0)
                def _():
                    @pl.loop(0, slots - 1)
                    def _(j):
                        wo_s[j + 1, pl.ds(pl.multiple_of(row, 32), r)] = stage[at, j].astype(BF)

            return put

        jobs = [(w1_pieces[n], None, store_out(n)) for n in range(8)]
        for n in range(8):
            jobs.append((w2_pieces[n].at[:, pl.ds(0, r)], None, store(wu_s, n)))
            jobs.append((w2_pieces[n].at[:, pl.ds(r, r)], None, store(wd_s, n)))
        fetch(jobs, stage, sems, 4)
        gall_ref[...] = jnp.zeros_like(gall_ref)
        sm_s[...] = jnp.zeros_like(sm_s)
        for c in own:
            c.wait()

    @pl.when(i < long0)
    def _():
        x_s[...] = xs_ref[...]
        c_s[...] = cs_ref[...]

    @pl.when(i >= long0)
    def _():
        x_s[...] = xl_ref[...]
        c_s[...] = cl_ref[...]

    def vec(n):
        return vec_ref[n : n + 1].astype(F32)

    attn = dot(o_ref[0], wo_s[0])
    for j in range(1, slots):
        attn = attn + dot(o_ref[j], wo_s[j])
    xhat1, rstd1 = norm_stats(x_s[...].astype(F32) + attn + vec(0))
    y1 = xhat1 * vec(2) + vec(4)
    y1b = y1.astype(BF)
    ffn = jnp.zeros_like(y1)
    for j in range(slots):
        u = dot(y1b, wu_s[j]) + bup_ref[j : j + 1]
        g, gp = gelu_both(u)
        gb = g.astype(BF)
        g_s[j] = gb
        gp_s[j] = gp
        ffn = ffn + dot(gb, wd_s[j])
    xhat2, rstd2 = norm_stats(y1 + ffn + vec(1))
    enc = (xhat2 * vec(3) + vec(5)).astype(BF)

    @pl.when(i < long0)
    def _():
        es_ref[...] = enc

    @pl.when(i >= long0)
    def _():
        el_ref[...] = enc

    dy = c_s[...].astype(F32)
    dh2 = norm_back(dy, xhat2, rstd2, vec(3))
    dz = dh2.astype(BF)
    sm_s[1] += row8(dh2)
    sm_s[3] += row8(dy * xhat2)
    sm_s[5] += row8(dy)
    dy1 = dh2
    for j in range(slots):
        du = (dot(dz, wd_s[j], NT) * gp_s[j]).astype(BF)
        du_s[j] = du
        dy1 = dy1 + dot(du, wu_s[j], NT)
    gall_ref[:, 0:fl] += dot(y1b, du_s[0], TN)
    gall_ref[:, fl : 2 * fl] += dot(dz, g_s[0], TN)
    sm_s[6] += row8(du_s[0].astype(F32))
    dh1 = norm_back(dy1, xhat1, rstd1, vec(2))
    dh_ref[...] = dh1
    da = dh1.astype(BF)
    sm_s[0] += row8(dh1)
    sm_s[2] += row8(dy1 * xhat1)
    sm_s[4] += row8(dy1)
    gall_ref[:, 2 * fl : 2 * fl + 256] += dot(da, o_ref[0], TN)
    for j in range(slots):
        do_ref[j] = dot(da, wo_s[j], NT).astype(BF)

    @pl.when(i == pl.num_programs(0) - 1)
    def _():
        small = jnp.sum(sm_s[...], axis=1)
        small = jnp.concatenate([small, jnp.zeros((120, d), F32)], 0)
        gall_ref[:, 2 * fl + 256 :] = small.T


def ffn_block(place, xs, xl, cs, cl, o, vecs, bup, own, pieces, hw, blk):
    srows, d = xs.shape
    rows = srows + xl.shape[0]
    slots = o.shape[0]
    fl = own[1].shape[1]
    r = pieces[0].shape[1]
    long0 = srows // blk
    row = lambda i, *_: (i, 0)
    grp = lambda i, *_: (0, i, 0)
    const = lambda i, *_: (0, 0)
    return pl.pallas_call(
        lambda *r: ffn_kernel(*r, long0=long0, hw=hw),
        grid_spec=pltpu.PrefetchScalarGridSpec(
            num_scalar_prefetch=1,
            grid=(rows // blk,),
            in_specs=blocks(blk, d, long0)
            + blocks(blk, d, long0)
            + [
                pl.BlockSpec((slots, blk, 256), grp),
                pl.BlockSpec((8, d), const),
                pl.BlockSpec((slots, fl), const),
            ]
            + [pl.BlockSpec(memory_space=pl.ANY)] * 19,
            out_specs=blocks(blk, d, long0)
            + [
                pl.BlockSpec((blk, d), row),
                pl.BlockSpec((slots, blk, 256), grp),
                pl.BlockSpec((d, 2 * fl + 384), const, pipeline_mode=pl.Buffered(1)),
            ],
            scratch_shapes=[
                pltpu.VMEM((slots, 256, d), BF),
                pltpu.VMEM((slots, d, fl), BF),
                pltpu.VMEM((slots, fl, d), BF),
                pltpu.VMEM((4, slots - 1, r, d), F32),
                pltpu.SemaphoreType.DMA((4,)),
                pltpu.SemaphoreType.DMA((3,)),
                pltpu.VMEM((slots, blk, fl), BF),
                pltpu.VMEM((slots, blk, fl), F32),
                pltpu.VMEM((slots, blk, fl), BF),
                pltpu.VMEM((8, 8, d), F32),
                pltpu.VMEM((blk, d), BF),
                pltpu.VMEM((blk, d), BF),
            ],
        ),
        out_shape=[
            jax.ShapeDtypeStruct((srows, d), BF),
            jax.ShapeDtypeStruct((rows - srows, d), BF),
            jax.ShapeDtypeStruct((rows, d), F32),
            jax.ShapeDtypeStruct((slots, rows, 256), BF),
            jax.ShapeDtypeStruct((d, 2 * fl + 384), F32),
        ],
        compiler_params=pltpu.CompilerParams(vmem_limit_bytes=62 * 2**20),
        cost_estimate=pl.CostEstimate(flops=80 * 10**9, bytes_accessed=2**25, transcendentals=0),
        name="ffn_block",
    )(place, xs, xl, cs, cl, o, vecs, bup, *own, *pieces)


class Wires:
    def __init__(self, n_dp, n_tensor):
        self.n_dp, self.n_tensor = n_dp, n_tensor
        self.first = [(i, i ^ (4 if i & 1 else 2)) for i in range(n_dp)]
        self.second = [(i, i ^ (2 if i & 1 else 4)) for i in range(n_dp)]
        self.pair = [(i, i ^ 1) for i in range(n_dp)]
        me = lax.axis_index("dp")
        odd = (me & 1).astype(jnp.int32)
        a, b = 2 + 2 * odd, 4 - 2 * odd
        masks = [0, a, b, 6, 1, 1 ^ b, 1 ^ a, 7]
        self.low = (me & 7).astype(jnp.int32)
        self.odd, self.x, self.y = odd, (self.low >> 1) & 1, self.low >> 2
        self.source = jnp.stack([jnp.asarray(self.low ^ m, jnp.int32) for m in masks])

    def piece(self, shard):
        extra = self.n_dp // 8
        r = shard.shape[0] // self.n_dp
        at = (self.low * extra + lax.axis_index("dp") // 8) * r
        return lax.dynamic_slice_in_dim(shard, at, r, 0).astype(F32)

    def along_tensor(self, piece):
        n = self.n_tensor
        return [
            lax.ppermute(piece, "tensor", [(i, (i + s) % n) for i in range(n)]) for s in range(1, n)
        ]

    def whole_eighth(self, z):
        if self.n_dp == 8:
            return z
        groups = [[g + 8 * e for e in range(self.n_dp // 8)] for g in range(8)]
        return lax.all_gather(z, "dp", axis=z.ndim - 2, tiled=True, axis_index_groups=groups)

    def first_hop(self, z):
        return lax.ppermute(z, "dp", self.first), lax.ppermute(z, "dp", self.second)

    def second_hop(self, a):
        return lax.ppermute(a, "dp", self.second)

    def to_pair(self, x):
        return lax.ppermute(x, "dp", self.pair)


    def split(self, g):
        rows, width = g.shape
        return g.reshape(self.n_dp // 8, 4, 2, rows // self.n_dp, width)

    def halve_pair(self, g):
        return self.to_pair(lax.dynamic_index_in_dim(g, 1 - self.odd, 2, keepdims=False))

    def sum_pair(self, g, got):
        return lax.dynamic_index_in_dim(g, self.odd, 2, keepdims=False) + got

    def two(self, h, x, y):
        n = jnp.where(self.odd == 1, 2 * y, x)
        m = jnp.where(self.odd == 1, 2 * y + 1, x + 2)
        return jnp.concatenate([lax.dynamic_slice_in_dim(h, i, 1, 1) for i in (n, m)], 1)

    def halve_first(self, h):
        return lax.ppermute(self.two(h, 1 - self.x, 1 - self.y), "dp", self.first)

    def sum_first(self, h, got):
        return self.two(h, self.x, self.y) + got

    def halve_second(self, k):
        at = jnp.where(self.odd == 1, self.x, self.y)
        return lax.ppermute(lax.dynamic_index_in_dim(k, 1 - at, 1, keepdims=False), "dp", self.second)

    def sum_second(self, k, got):
        at = jnp.where(self.odd == 1, self.x, self.y)
        out = lax.dynamic_index_in_dim(k, at, 1, keepdims=False) + got
        if self.n_dp == 8:
            return out[0]
        groups = [[g + 8 * e for e in range(self.n_dp // 8)] for g in range(8)]
        return lax.psum_scatter(out, "dp", scatter_dimension=0, axis_index_groups=groups)


def after(x, *others):
    return lax.optimization_barrier((x, *others))[0]


def make(n_dp, n_tensor):
    def on_device(
        short_tokens,
        short_lengths,
        long_tokens,
        long_lengths,
        w_qkv,
        b_qv,
        w_out,
        res_biases,
        ln_gains,
        ln_shifts,
        w_up,
        b_up,
        w_down,
        short_cotangent,
        long_cotangent,
    ):
        ns, ss, d = short_tokens.shape
        nl, ls, _ = long_tokens.shape
        srows = ns * ss
        heads, hd = b_qv.shape[1], b_qv.shape[2]
        hw = heads * hd
        blk = ls
        kw = dict(nshort=ns, short_slot=ss, heads=heads, blk=blk)
        wires = Wires(n_dp, n_tensor)
        r = w_up.shape[0] // 8

        w1_own = jnp.concatenate([w_qkv.transpose(0, 2, 1).reshape(3 * hw, d), w_out], 0)
        tail = jnp.zeros((d - 2 * hw,), F32)
        small = jnp.stack([b_up[0].astype(F32), jnp.concatenate([b_qv.reshape(2 * hw).astype(F32), tail])])
        small = jnp.concatenate([small, jnp.zeros((6, d), F32)], 0)
        piece = wires.piece(w1_own)
        pr = piece.shape[0]
        z = wires.along_tensor(jnp.concatenate([small, piece], 0))
        row = wires.source * r
        c = row // hw
        place = jnp.stack(
            [row, jnp.where(c < 3, c * 256 + row - c * hw, -1), jnp.where(c < 3, -1, row - 3 * hw)]
        )

        one = np.zeros((256 - hw,), np.float32)
        one[1 : 1 + 3 * heads] = 1.0
        one = jnp.asarray(one)

        def bias_of(sm):
            zero = jnp.zeros((256 - hw,), F32)
            none = jnp.zeros((hw,), F32)
            return jnp.concatenate([sm[1, :hw], zero, none, one, sm[1, hw : 2 * hw], one])[None]

        xs, xl = short_tokens.reshape(srows, d), long_tokens.reshape(-1, d)
        cs, cl = short_cotangent.reshape(srows, d), long_cotangent.reshape(-1, d)
        lens = jnp.concatenate([short_lengths, long_lengths])
        po = attn_fwd(0, lens, place, xs, xl, w1_own, bias_of(small), None, slots=n_tensor, **kw)

        t1 = wires.whole_eighth(after(jnp.stack([x[8:] for x in z]), po[1]))
        a1, b1 = wires.first_hop(t1)
        piece2 = after(jnp.stack([wires.piece(w_up), wires.piece(w_down)]), po[1])
        z2 = wires.along_tensor(piece2)
        c1 = wires.second_hop(after(a1, z2[0]))
        w1 = [t1, a1, b1, c1]
        w1 += [wires.to_pair(x) for x in w1[:3]] + [wires.to_pair(after(c1, z2[2]))]
        def eighths(*x):
            return wires.whole_eighth(jnp.stack(x)).reshape(len(x), -1, d)

        t2 = eighths(z2[0], z2[2])
        a2, b2 = wires.first_hop(t2)
        for s in range(1, n_tensor):
            po = attn_fwd(s, lens, place, xs, xl, w1, bias_of(z[s - 1]), po, slots=n_tensor, **kw)
            if s == 1:
                a2, b2, mid, *po = lax.optimization_barrier((a2, b2, z2[1], *po))
                t2b = eighths(mid)
                a2b, b2b = wires.first_hop(t2b)
            if s == 2:
                a2b, b2b, *po = lax.optimization_barrier((a2b, b2b, *po))
                t2, a2, b2 = [
                    jnp.concatenate([u[:1], v, u[1:]], 0)
                    for u, v in ((t2, t2b), (a2, a2b), (b2, b2b))
                ]
                c2 = wires.second_hop(a2)
        c2, *po = lax.optimization_barrier((c2, *po))
        w2 = [t2, a2, b2, c2]
        w2 += [wires.to_pair(x) for x in w2]
        p, o = po
        bup = jnp.stack([x[0] for x in [small] + z])
        vecs = jnp.concatenate([res_biases, ln_gains, ln_shifts, jnp.zeros((2, d), BF)], 0).astype(F32)
        es, el, dh, do, gall = ffn_block(
            place, xs, xl, cs, cl, o, vecs, bup, [w1_own, w_up, w_down], w1 + w2, hw, 256
        )
        fl = w_up.shape[1]
        gall = wires.split(gall)
        got = wires.halve_pair(gall)
        dp_own, gw, gb = bwd_own(xs, xl, p, o, do, **kw)
        gall = wires.sum_pair(gall, after(got, dp_own))
        got = wires.halve_first(gall)
        gb = gb.sum(0).reshape(3, 256)
        gb = jnp.stack([gb[0, :hw], gb[2, :hw]]).reshape(2 * heads, n_dp, hd // n_dp)
        gb = gb.transpose(1, 0, 2).reshape(n_dp, 1, -1)
        gw = lax.dynamic_update_slice(gw.reshape(n_dp, d // n_dp, 768), gb, (0, 0, hw))
        gw = wires.split(gw.reshape(d, 768))
        gotw = wires.halve_pair(gw)
        nb = (ns * ss + nl * ls) // blk
        rest = (place, p, o, do, dp_own, dh, w1_own, w1, srows)
        gs, gl = bwd_rest(0, nb // 2, None, *rest, **kw)
        got, gotw, gl = lax.optimization_barrier((got, gotw, gl))
        gall = wires.sum_first(gall, got)
        got = wires.halve_second(gall)
        gw = wires.sum_pair(gw, gotw)
        gotw = wires.halve_first(gw)
        (gl,) = bwd_rest(nb // 2, nb, gl, *rest, **kw)
        got, gotw, gl = lax.optimization_barrier((got, gotw, gl))
        gw = wires.sum_first(gw, gotw)
        gotw = wires.halve_second(gw)
        gall = wires.sum_second(gall, got)
        gw = wires.sum_second(gw, gotw)
        small_shard = gall[:, 2 * fl + 256 : 2 * fl + 264].T
        gqkv = gw.reshape(-1, 3, 256)[:, :, :hw].transpose(1, 0, 2)
        qv_shard = gw[0, hw : hw + 2 * hw // n_dp].reshape(2, heads, hd // n_dp)
        return (
            es.reshape(ns, ss, d),
            el.reshape(nl, ls, d),
            gs.reshape(ns, ss, d),
            gl.reshape(nl, ls, d),
            gqkv,
            qv_shard,
            gall[:, 2 * fl : 2 * fl + hw].T,
            small_shard[0:2],
            small_shard[2:4],
            small_shard[4:6],
            gall[:, :fl],
            small_shard[6:7],
            gall[:, fl : 2 * fl].T,
        )

    return on_device


def solution(mesh):
    tok = P("dp", None, None)
    return jax.shard_map(
        make(mesh.shape["dp"], mesh.shape["tensor"]),
        mesh=mesh,
        in_specs=(
            tok,
            P("dp"),
            tok,
            P("dp"),
            P(None, None, "tensor"),
            P(None, "tensor", None),
            P("tensor", None),
            P(),
            P(),
            P(),
            P(None, "tensor"),
            P("tensor", None),
            P("tensor", None),
            tok,
            tok,
        ),
        out_specs=(
            tok,
            tok,
            tok,
            tok,
            P(None, "dp", "tensor"),
            P(None, "tensor", "dp"),
            P("tensor", "dp"),
            P(None, "dp"),
            P(None, "dp"),
            P(None, "dp"),
            P("dp", "tensor"),
            P("tensor", "dp"),
            P("tensor", "dp"),
        ),
        check_vma=False,
    )
```

```python
import jax
import jax.numpy as jnp
import numpy as np
from jax import lax
from jax.experimental import pallas as pl
from jax.experimental.pallas import tpu as pltpu
from jax.sharding import PartitionSpec as P

HD = 64
EPS = 1e-12
BF = jnp.bfloat16
F32 = jnp.float32
NT = (((1,), (1,)), ((), ()))
TN = (((0,), (0,)), ((), ()))


def dot(a, b, dims=(((1,), (0,)), ((), ()))):
    return lax.dot_general(a, b, dims, preferred_element_type=F32)


def lanes(width, test):
    lane = lax.broadcasted_iota(jnp.int32, (1, width), 1)
    return jnp.where(test(lane), 1.0, 0.0).astype(F32)


def head_row(h, width, extra):
    w = width * HD

    def test(lane):
        own = (lane >= h * HD) & (lane < (h + 1) * HD)
        if extra:
            own = own | ((lane >= w + 1 + 3 * h) & (lane < w + 4 + 3 * h))
        return own

    return test


def split3(x):
    hi = x.astype(BF).astype(F32)
    rest = x - hi
    mid = rest.astype(BF).astype(F32)
    return hi, mid, rest - mid


def blocks(blk, d, nshort, grid_pos=0):
    return [
        pl.BlockSpec((blk, d), lambda *g: (jnp.minimum(g[grid_pos], nshort - 1), 0)),
        pl.BlockSpec((blk, d), lambda *g: (jnp.maximum(g[grid_pos] - nshort, 0), 0)),
    ]


def fetch(jobs, stage, sems, depth):
    def copy(n):
        src, idx, _ = jobs[n]
        dst = stage.at[n % depth] if idx is None else stage.at[n % depth, idx]
        return pltpu.make_async_copy(src, dst, sems.at[n % depth])

    for n in range(min(depth - 1, len(jobs))):
        copy(n).start()
    for n in range(len(jobs)):
        if n + depth - 1 < len(jobs):
            copy(n + depth - 1).start()
        copy(n).wait()
        jobs[n][2](n % depth)


def attn_fwd_kernel(
    len_ref, place_ref, slot_ref, xs_ref, xl_ref, b_ref, *refs, own, nshort, short_slot, heads, blk
):
    if not own:
        pieces, (p_ref, o_ref, w_s, x_s, stage, sems) = refs[:8], refs[-6:]
    else:
        w_ref, p_ref, o_ref, w_s, x_s = refs
    hw = heads * HD
    b = pl.program_id(0)
    sub = blk // short_slot
    long0 = nshort // sub

    @pl.when(b == 0)
    def _():
        if not own:
            at = slot_ref[0] - 1
            copies = [
                pltpu.make_async_copy(pieces[n].at[at], stage.at[n], sems.at[n])
                for n in range(8)
            ]
            for c in copies:
                c.start()
            w_s[...] = jnp.zeros_like(w_s)
            r = stage.shape[1]
            for n in range(8):
                copies[n].wait()
                row = place_ref[1, n]

                @pl.when(row >= 0)
                def _():
                    w_s[pl.ds(pl.multiple_of(row, 32), r)] = stage[n].astype(BF)

        else:
            w_s[...] = jnp.zeros_like(w_s)
            for c in range(3):
                w_s[256 * c : 256 * c + hw] = w_ref[c * hw : (c + 1) * hw]

    @pl.when(b < long0)
    def _():
        x_s[...] = xs_ref[...]

    @pl.when(b >= long0)
    def _():
        x_s[...] = xl_ref[...]

    p_ref[0] = (dot(x_s[...], w_s[...], NT) + b_ref[...]).astype(BF)

    def pair(row, rows, length):
        sl = pl.ds(row, rows)
        pos = lax.broadcasted_iota(jnp.int32, (rows, 1), 0)
        hidden = jnp.where(pos < length, 0.0, -1e30)
        at_mask = lanes(256, lambda l: l == hw)
        q = (p_ref[0, sl, 0:256].astype(F32) * 0.125 + at_mask).astype(BF)
        k = (p_ref[0, sl, 256:512].astype(F32) + hidden * at_mask).astype(BF)
        v = p_ref[0, sl, 512:768]
        p_ref[0, sl, 256:512] = k
        out = jnp.zeros((rows, 256), F32)
        ext = jnp.zeros((rows, 256), F32)
        for h in range(heads):
            own = lanes(256, head_row(h, heads, False))
            s = dot(q * (own + at_mask).astype(BF), k, NT)
            m = jnp.max(s, axis=1, keepdims=True)
            e = jnp.exp(s - m)
            total = jnp.sum(e, axis=1, keepdims=True)
            a = (e * (1.0 / total)).astype(BF)
            out = out + dot(a, v * own.astype(BF))
            for i, part in enumerate(split3(-(m + jnp.log(total)))):
                ext = ext + part * lanes(256, lambda l: l == hw + 1 + 3 * h + i)
        p_ref[0, sl, 0:256] = (q.astype(F32) + ext).astype(BF)
        o_ref[0, sl] = out.astype(BF)

    @pl.when(b < long0)
    def _():
        @pl.loop(0, sub)
        def _(i):
            pair(pl.multiple_of(i * short_slot, short_slot), short_slot, len_ref[b * sub + i])

    @pl.when(b >= long0)
    def _():
        pair(0, blk, len_ref[nshort + b - long0])


def attn_fwd(slot, lens, place, xs, xl, w, bias, prev, nshort, short_slot, heads, blk, slots):
    rows, d = xs.shape[0] + xl.shape[0], xs.shape[1]
    in_specs = blocks(blk, d, xs.shape[0] // blk) + [pl.BlockSpec((1, 768), lambda b, *_: (0, 0))]
    args = [xs, xl, bias]
    scratch = [pltpu.VMEM((768, d), BF), pltpu.VMEM((blk, d), BF)]
    aliases = {}
    if slot:
        in_specs += [pl.BlockSpec(memory_space=pl.ANY)] * 10
        args += list(w) + list(prev)
        aliases = {14: 0, 15: 1}
        r = w[0].shape[1]
        scratch += [pltpu.VMEM((8, r, d), F32), pltpu.SemaphoreType.DMA((8,))]
    else:
        in_specs.append(pl.BlockSpec(w.shape, lambda b, *_: (0, 0)))
        args.append(w)
    return pl.pallas_call(
        lambda *r: attn_fwd_kernel(
            *r, own=slot == 0, nshort=nshort, short_slot=short_slot, heads=heads, blk=blk
        ),
        grid_spec=pltpu.PrefetchScalarGridSpec(
            num_scalar_prefetch=3,
            grid=(rows // blk,),
            in_specs=in_specs,
            out_specs=[
                pl.BlockSpec((1, blk, 768), lambda b, ln, at, sl: (sl[0], b, 0)),
                pl.BlockSpec((1, blk, 256), lambda b, ln, at, sl: (sl[0], b, 0)),
            ],
            scratch_shapes=scratch,
        ),
        out_shape=[
            jax.ShapeDtypeStruct((slots, rows, 768), BF),
            jax.ShapeDtypeStruct((slots, rows, 256), BF),
        ],
        input_output_aliases=aliases,
        compiler_params=pltpu.CompilerParams(vmem_limit_bytes=60 * 2**20),
        cost_estimate=pl.CostEstimate(flops=14 * 10**9, bytes_accessed=2**23, transcendentals=0),
        name="attn_fwd",
    )(lens, place, jnp.full((1,), slot, jnp.int32), *args)


def attn_bwd_pair(refs, sl, rows, heads):
    p_ref, o_ref, do_ref = refs
    hw = heads * HD
    q, k, v = p_ref[0, sl, 0:256], p_ref[0, sl, 256:512], p_ref[0, sl, 512:768]
    do = do_ref[0, sl]
    do32 = do.astype(F32)
    prod = do32 * o_ref[0, sl].astype(F32)
    ext = do32
    for h in range(heads):
        own = lanes(256, head_row(h, heads, False))
        delta = jnp.sum(prod * own, axis=1, keepdims=True)
        for i, part in enumerate(split3(-delta)):
            ext = ext + part * lanes(256, lambda l: l == hw + 1 + 3 * h + i)
    do_ext = ext.astype(BF)
    kt = k.T
    at_mask = lanes(256, lambda l: l == hw)
    dk = jnp.zeros((rows, 256), F32)
    dv = jnp.zeros((rows, 256), F32)
    dqs = []
    for h in range(heads):
        row = lanes(256, head_row(h, heads, True))
        qh = q * (row + at_mask).astype(BF)
        doh = do_ext * row.astype(BF)
        p = jnp.exp(dot(k, qh, NT))
        ds = (p * dot(v, doh, NT)).astype(BF)
        dv = dv + dot(p.astype(BF), doh)
        dk = dk + dot(ds, qh)
        dqs.append(dot(kt[h * HD : (h + 1) * HD], ds))
    dqs.append(jnp.zeros((256 - hw, rows), F32))
    dq = jnp.concatenate(dqs, 0).T * 0.125
    real = lanes(256, lambda l: l < hw)
    return dq.astype(BF), (dk * real).astype(BF), (dv * real).astype(BF)


def over_pairs(b, refs, dst, *, nshort, short_slot, heads, blk):
    sub = blk // short_slot
    long0 = nshort // sub

    def one(row, rows):
        sl = pl.ds(row, rows)
        for c, val in enumerate(attn_bwd_pair(refs, sl, rows, heads)):
            dst(sl, c, val)

    @pl.when(b < long0)
    def _():
        @pl.loop(0, sub)
        def _(i):
            one(pl.multiple_of(i * short_slot, short_slot), short_slot)

    @pl.when(b >= long0)
    def _():
        one(0, blk)


def bwd_own_kernel(
    xs_ref, xl_ref, p_ref, o_ref, do_ref, dp_ref, gw_ref, gb_ref, *, n_dp, **kw
):
    b = pl.program_id(0)
    long0 = kw["nshort"] * kw["short_slot"] // kw["blk"]

    def dst(sl, c, val):
        dp_ref[sl, 256 * c : 256 * (c + 1)] = val

    over_pairs(b, (p_ref, o_ref, do_ref), dst, **kw)

    @pl.when(b == 0)
    def _():
        gw_ref[...] = jnp.zeros_like(gw_ref)
        gb_ref[...] = jnp.zeros_like(gb_ref)

    @pl.when(b < long0)
    def _():
        gw_ref[...] += dot(xs_ref[...], dp_ref[...], TN)

    @pl.when(b >= long0)
    def _():
        gw_ref[...] += dot(xl_ref[...], dp_ref[...], TN)

    gb_ref[...] += jnp.sum(dp_ref[...].astype(F32).reshape(-1, 8, 768), axis=0)

    @pl.when(b == pl.num_programs(0) - 1)
    def _():
        d, heads = gw_ref.shape[0], kw["heads"]
        hw, r, part = heads * HD, d // n_dp, HD // n_dp
        total = jnp.sum(gb_ref[...], axis=0, keepdims=True)
        row = lax.broadcasted_iota(jnp.int32, (d, 1), 0)
        owner = sum((row >= i * r).astype(jnp.int32) for i in range(1, n_dp))
        k = row - owner * r
        h = sum((k >= i * part).astype(jnp.int32) for i in range(1, heads + 1))
        n = jnp.where(h < heads, h * HD + owner * part + k - h * part, -1)
        lane = lax.broadcasted_iota(jnp.int32, (1, 256), 1)
        spare = lane[:, 128:]

        def column(v):
            return jnp.sum(jnp.where(lane == n, v, 0.0), axis=1, keepdims=True)

        gw_ref[:, 128:256] += jnp.where(
            spare == hw,
            column(total[:, 0:256]),
            jnp.where(spare == hw + 1, column(total[:, 512:768]), 0.0),
        )


def bwd_own(xs, xl, p, o, do, blk, **kw):
    rows, d = xs.shape[0] + xl.shape[0], xs.shape[1]
    return pl.pallas_call(
        lambda *r: bwd_own_kernel(*r, blk=blk, **kw),
        grid=(rows // blk,),
        in_specs=blocks(blk, d, xs.shape[0] // blk)
        + [
            pl.BlockSpec((1, blk, 768), lambda b: (0, b, 0)),
            pl.BlockSpec((1, blk, 256), lambda b: (0, b, 0)),
            pl.BlockSpec((1, blk, 256), lambda b: (0, b, 0)),
        ],
        out_specs=[
            pl.BlockSpec((blk, 768), lambda b: (b, 0)),
            pl.BlockSpec((d, 768), lambda b: (0, 0)),
        ],
        out_shape=[
            jax.ShapeDtypeStruct((rows, 768), BF),
            jax.ShapeDtypeStruct((d, 768), F32),
        ],
        scratch_shapes=[pltpu.VMEM((8, 768), F32)],
        compiler_params=pltpu.CompilerParams(vmem_limit_bytes=60 * 2**20),
        cost_estimate=pl.CostEstimate(flops=18 * 10**9, bytes_accessed=2**23, transcendentals=0),
        name="attn_bwd_own",
    )(xs, xl, p, o, do)


def bwd_rest_kernel(
    place_ref, p_ref, o_ref, do_ref, own_ref, dh_ref, w_hbm, *refs, lo, **kw
):
    pieces, gs_ref, (gl_ref, dp_s, w_s, stage, sems, sem) = refs[:8], refs[8], refs[-6:]
    b, g = pl.program_id(0) + lo, pl.program_id(1)
    slots = w_s.shape[0]
    hw = kw["heads"] * HD
    long0 = kw["nshort"] * kw["short_slot"] // kw["blk"]

    @pl.when((b == lo) & (g == 0))
    def _():
        own = [
            pltpu.make_async_copy(
                w_hbm.at[pl.ds(c * hw, hw)], w_s.at[0, pl.ds(256 * c, hw)], sem.at[c]
            )
            for c in range(3)
        ]
        w_s[...] = jnp.zeros_like(w_s)
        for c in own:
            c.start()

        def store(n):
            def put(at):
                row = place_ref[1, n]

                @pl.when(row >= 0)
                def _():
                    @pl.loop(0, slots - 1)
                    def _(j):
                        w_s[j + 1, pl.ds(pl.multiple_of(row, 32), stage.shape[2])] = stage[
                            at, j
                        ].astype(BF)

            return put

        fetch([(pieces[n], None, store(n)) for n in range(8)], stage, sems, 3)
        for c in own:
            c.wait()

    @pl.when(g == 0)
    def _():
        dp_s[0] = own_ref[...]

    def dst(sl, c, val):
        dp_s[g + 1, sl, 256 * c : 256 * (c + 1)] = val

    over_pairs(b, (p_ref, o_ref, do_ref), dst, **kw)

    @pl.when(g == slots - 2)
    def _():
        acc = dh_ref[...]
        for j in range(slots):
            acc = acc + dot(dp_s[j], w_s[j])

        if lo < long0:

            @pl.when(b < long0)
            def _():
                gs_ref[...] = acc

        @pl.when(b >= long0)
        def _():
            gl_ref[...] = acc


def bwd_rest(lo, hi, prev, place, p, o, do, own_dp, dh, w_own, pieces, srows, blk, **kw):
    slots, rows, _ = p.shape
    d = dh.shape[1]
    r = pieces[0].shape[1]

    long0 = srows // blk
    assert lo == 0 or lo >= long0
    last = lo > 0

    def grp_map(b, g, *_):
        return (g + 1, b + lo, 0)

    return pl.pallas_call(
        lambda *r: bwd_rest_kernel(*r, lo=lo, blk=blk, **kw),
        grid_spec=pltpu.PrefetchScalarGridSpec(
            num_scalar_prefetch=1,
            grid=(hi - lo, slots - 1),
            in_specs=[
                pl.BlockSpec((1, blk, 768), grp_map),
                pl.BlockSpec((1, blk, 256), grp_map),
                pl.BlockSpec((1, blk, 256), grp_map),
                pl.BlockSpec((blk, 768), lambda b, g, *_: (b + lo, 0)),
                pl.BlockSpec((blk, d), lambda b, g, *_: (b + lo, 0)),
            ]
            + [pl.BlockSpec(memory_space=pl.ANY)] * (9 + last),
            out_specs=[pl.BlockSpec((blk, d), lambda b, g, *_: (b + lo - long0, 0))]
            if last
            else blocks(blk, d, long0),
            scratch_shapes=[
                pltpu.VMEM((slots, blk, 768), BF),
                pltpu.VMEM((slots, 768, d), BF),
                pltpu.VMEM((3, slots - 1, r, d), F32),
                pltpu.SemaphoreType.DMA((3,)),
                pltpu.SemaphoreType.DMA((3,)),
            ],
        ),
        out_shape=[
            jax.ShapeDtypeStruct((srows, d), F32),
            jax.ShapeDtypeStruct((rows - srows, d), F32),
        ][last:],
        input_output_aliases={15: 0} if last else {},
        compiler_params=pltpu.CompilerParams(vmem_limit_bytes=60 * 2**20),
        cost_estimate=pl.CostEstimate(flops=25 * 10**9, bytes_accessed=2**23, transcendentals=0),
        name="attn_bwd_rest",
    )(place, p, o, do, own_dp, dh, w_own, *pieces, *([prev] if last else []))


def norm_stats(h):
    center = h - jnp.mean(h, -1, keepdims=True)
    rstd = lax.rsqrt(jnp.mean(center * center, -1, keepdims=True) + EPS)
    return center * rstd, rstd


def norm_back(dy, xhat, rstd, gain):
    s = dy * gain
    return rstd * (
        s - jnp.mean(s, -1, keepdims=True) - xhat * jnp.mean(s * xhat, -1, keepdims=True)
    )


def gelu_both(u):
    phi = 0.5 + 0.5 * lax.erf(u * 0.7071067811865476)
    pdf = jnp.exp2(u * u * (-0.5 * 1.4426950408889634)) * 0.3989422804014327
    return u * phi, phi + u * pdf


def row8(x):
    return jnp.sum(x.reshape(-1, 8, x.shape[-1]), axis=0)


def ffn_kernel(place_ref, *refs, long0, hw):
    (xs_ref, xl_ref, cs_ref, cl_ref, o_ref, vec_ref, bup_ref, w1_hbm, wu_hbm, wd_hbm) = refs[:10]
    w1_pieces, w2_pieces = refs[10:18], refs[18:26]
    (es_ref, el_ref, dh_ref, do_ref, gall_ref) = refs[26:31]
    (wo_s, wu_s, wd_s, stage, sems, sem, g_s, gp_s, du_s, sm_s, x_s, c_s) = refs[31:]
    i = pl.program_id(0)
    slots, d, fl = wu_s.shape
    r = stage.shape[2]

    @pl.when(i == 0)
    def _():
        wo_s[...] = jnp.zeros_like(wo_s)
        own = [
            pltpu.make_async_copy(wu_hbm, wu_s.at[0], sem.at[0]),
            pltpu.make_async_copy(wd_hbm, wd_s.at[0], sem.at[1]),
            pltpu.make_async_copy(
                w1_hbm.at[pl.ds(3 * hw, hw)], wo_s.at[0, pl.ds(0, hw)], sem.at[2]
            ),
        ]
        for c in own:
            c.start()

        def store(dst, n):
            def put(at):
                row = pl.multiple_of(place_ref[0, n], 32)

                @pl.loop(0, slots - 1)
                def _(j):
                    dst[j + 1, pl.ds(row, r)] = stage[at, j].astype(BF)

            return put

        def out_rows(n, do):
            row = place_ref[2, n]

            @pl.when(row >= 0)
            def _():
                at = row // r
                do(pltpu.make_async_copy(w1_pieces[n], stage.at[at], sems.at[at]), at, row)

        def store_out(copy, at, row):
            copy.wait()

            @pl.loop(0, slots - 1)
            def _(j):
                wo_s[j + 1, pl.ds(pl.multiple_of(row, 32), r)] = stage[at, j].astype(BF)

        for n in range(8):
            out_rows(n, lambda copy, at, row: copy.start())
        for n in range(8):
            out_rows(n, store_out)
        jobs = []
        for n in range(8):
            jobs.append((w2_pieces[n].at[:, pl.ds(0, r)], None, store(wu_s, n)))
            jobs.append((w2_pieces[n].at[:, pl.ds(r, r)], None, store(wd_s, n)))
        fetch(jobs, stage, sems, 4)
        gall_ref[...] = jnp.zeros_like(gall_ref)
        sm_s[...] = jnp.zeros_like(sm_s)
        for c in own:
            c.wait()

    @pl.when(i < long0)
    def _():
        x_s[...] = xs_ref[...]
        c_s[...] = cs_ref[...]

    @pl.when(i >= long0)
    def _():
        x_s[...] = xl_ref[...]
        c_s[...] = cl_ref[...]

    def vec(n):
        return vec_ref[n : n + 1].astype(F32)

    attn = dot(o_ref[0], wo_s[0])
    for j in range(1, slots):
        attn = attn + dot(o_ref[j], wo_s[j])
    xhat1, rstd1 = norm_stats(x_s[...].astype(F32) + attn + vec(0))
    y1 = xhat1 * vec(2) + vec(4)
    y1b = y1.astype(BF)
    ffn = jnp.zeros_like(y1)
    for j in range(slots):
        u = dot(y1b, wu_s[j]) + bup_ref[j : j + 1]
        g, gp = gelu_both(u)
        gb = g.astype(BF)
        g_s[j] = gb
        gp_s[j] = gp
        ffn = ffn + dot(gb, wd_s[j])
    xhat2, rstd2 = norm_stats(y1 + ffn + vec(1))
    enc = (xhat2 * vec(3) + vec(5)).astype(BF)

    @pl.when(i < long0)
    def _():
        es_ref[...] = enc

    @pl.when(i >= long0)
    def _():
        el_ref[...] = enc

    dy = c_s[...].astype(F32)
    dh2 = norm_back(dy, xhat2, rstd2, vec(3))
    dz = dh2.astype(BF)
    sm_s[1] += row8(dh2)
    sm_s[3] += row8(dy * xhat2)
    sm_s[5] += row8(dy)
    dy1 = dh2
    for j in range(slots):
        du = (dot(dz, wd_s[j], NT) * gp_s[j]).astype(BF)
        du_s[j] = du
        dy1 = dy1 + dot(du, wu_s[j], NT)
    gall_ref[:, 0:fl] += dot(y1b, du_s[0], TN)
    gall_ref[:, fl : 2 * fl] += dot(dz, g_s[0], TN)
    sm_s[6] += row8(du_s[0].astype(F32))
    dh1 = norm_back(dy1, xhat1, rstd1, vec(2))
    dh_ref[...] = dh1
    da = dh1.astype(BF)
    sm_s[0] += row8(dh1)
    sm_s[2] += row8(dy1 * xhat1)
    sm_s[4] += row8(dy1)
    gall_ref[:, 2 * fl : 2 * fl + 256] += dot(da, o_ref[0], TN)
    for j in range(slots):
        do_ref[j] = dot(da, wo_s[j], NT).astype(BF)

    @pl.when(i == pl.num_programs(0) - 1)
    def _():
        small = jnp.sum(sm_s[...], axis=1)
        small = jnp.concatenate([small, jnp.zeros((120, d), F32)], 0)
        gall_ref[:, 2 * fl + 256 :] = small.T


def ffn_block(place, xs, xl, cs, cl, o, vecs, bup, own, pieces, hw, blk):
    srows, d = xs.shape
    rows = srows + xl.shape[0]
    slots = o.shape[0]
    fl = own[1].shape[1]
    r = pieces[0].shape[1]
    assert hw <= 4 * r
    long0 = srows // blk
    row = lambda i, *_: (i, 0)
    grp = lambda i, *_: (0, i, 0)
    const = lambda i, *_: (0, 0)
    return pl.pallas_call(
        lambda *r: ffn_kernel(*r, long0=long0, hw=hw),
        grid_spec=pltpu.PrefetchScalarGridSpec(
            num_scalar_prefetch=1,
            grid=(rows // blk,),
            in_specs=blocks(blk, d, long0)
            + blocks(blk, d, long0)
            + [
                pl.BlockSpec((slots, blk, 256), grp),
                pl.BlockSpec((8, d), const),
                pl.BlockSpec((slots, fl), const),
            ]
            + [pl.BlockSpec(memory_space=pl.ANY)] * 19,
            out_specs=blocks(blk, d, long0)
            + [
                pl.BlockSpec((blk, d), row),
                pl.BlockSpec((slots, blk, 256), grp),
                pl.BlockSpec((d, 2 * fl + 384), const, pipeline_mode=pl.Buffered(1)),
            ],
            scratch_shapes=[
                pltpu.VMEM((slots, 256, d), BF),
                pltpu.VMEM((slots, d, fl), BF),
                pltpu.VMEM((slots, fl, d), BF),
                pltpu.VMEM((4, slots - 1, r, d), F32),
                pltpu.SemaphoreType.DMA((4,)),
                pltpu.SemaphoreType.DMA((3,)),
                pltpu.VMEM((slots, blk, fl), BF),
                pltpu.VMEM((slots, blk, fl), F32),
                pltpu.VMEM((slots, blk, fl), BF),
                pltpu.VMEM((8, 8, d), F32),
                pltpu.VMEM((blk, d), BF),
                pltpu.VMEM((blk, d), BF),
            ],
        ),
        out_shape=[
            jax.ShapeDtypeStruct((srows, d), BF),
            jax.ShapeDtypeStruct((rows - srows, d), BF),
            jax.ShapeDtypeStruct((rows, d), F32),
            jax.ShapeDtypeStruct((slots, rows, 256), BF),
            jax.ShapeDtypeStruct((d, 2 * fl + 384), F32),
        ],
        compiler_params=pltpu.CompilerParams(vmem_limit_bytes=62 * 2**20),
        cost_estimate=pl.CostEstimate(flops=80 * 10**9, bytes_accessed=2**25, transcendentals=0),
        name="ffn_block",
    )(place, xs, xl, cs, cl, o, vecs, bup, *own, *pieces)


class Wires:
    def __init__(self, n_dp, n_tensor):
        self.n_dp, self.n_tensor = n_dp, n_tensor
        self.first = [(i, i ^ (4 if i & 1 else 2)) for i in range(n_dp)]
        self.second = [(i, i ^ (2 if i & 1 else 4)) for i in range(n_dp)]
        self.pair = [(i, i ^ 1) for i in range(n_dp)]
        me = lax.axis_index("dp")
        odd = (me & 1).astype(jnp.int32)
        a, b = 2 + 2 * odd, 4 - 2 * odd
        masks = [0, a, b, 6, 1, 1 ^ b, 1 ^ a, 7]
        self.low = (me & 7).astype(jnp.int32)
        self.odd, self.x, self.y = odd, (self.low >> 1) & 1, self.low >> 2
        self.source = jnp.stack([jnp.asarray(self.low ^ m, jnp.int32) for m in masks])

    def piece(self, shard):
        extra = self.n_dp // 8
        r = shard.shape[0] // self.n_dp
        at = (self.low * extra + lax.axis_index("dp") // 8) * r
        return lax.dynamic_slice_in_dim(shard, at, r, 0).astype(F32)

    def along_tensor(self, piece, shift):
        n = self.n_tensor
        return lax.ppermute(piece, "tensor", [(i, (i + shift) % n) for i in range(n)])

    def whole_eighth(self, z):
        if self.n_dp == 8:
            return z
        groups = [[g + 8 * e for e in range(self.n_dp // 8)] for g in range(8)]
        return lax.all_gather(z, "dp", axis=z.ndim - 2, tiled=True, axis_index_groups=groups)

    def first_hop(self, z):
        return lax.ppermute(z, "dp", self.first), lax.ppermute(z, "dp", self.second)

    def second_hop(self, a):
        return lax.ppermute(a, "dp", self.second)

    def to_pair(self, x):
        return lax.ppermute(x, "dp", self.pair)


    def split(self, g):
        rows, width = g.shape
        return g.reshape(self.n_dp // 8, 4, 2, rows // self.n_dp, width)

    def halve_pair(self, g):
        return self.to_pair(lax.dynamic_index_in_dim(g, 1 - self.odd, 2, keepdims=False))

    def sum_pair(self, g, got):
        return lax.dynamic_index_in_dim(g, self.odd, 2, keepdims=False) + got

    def two(self, h, x, y):
        n = jnp.where(self.odd == 1, 2 * y, x)
        m = jnp.where(self.odd == 1, 2 * y + 1, x + 2)
        return jnp.concatenate([lax.dynamic_slice_in_dim(h, i, 1, 1) for i in (n, m)], 1)

    def halve_first(self, h):
        return lax.ppermute(self.two(h, 1 - self.x, 1 - self.y), "dp", self.first)

    def sum_first(self, h, got):
        return self.two(h, self.x, self.y) + got

    def halve_second(self, k):
        at = jnp.where(self.odd == 1, self.x, self.y)
        return lax.ppermute(lax.dynamic_index_in_dim(k, 1 - at, 1, keepdims=False), "dp", self.second)

    def sum_second(self, k, got):
        at = jnp.where(self.odd == 1, self.x, self.y)
        out = lax.dynamic_index_in_dim(k, at, 1, keepdims=False) + got
        if self.n_dp == 8:
            return out[0]
        groups = [[g + 8 * e for e in range(self.n_dp // 8)] for g in range(8)]
        return lax.psum_scatter(out, "dp", scatter_dimension=0, axis_index_groups=groups)


def after(x, *others):
    return lax.optimization_barrier((x, *others))[0]


def make(n_dp, n_tensor):
    def on_device(
        short_tokens,
        short_lengths,
        long_tokens,
        long_lengths,
        w_qkv,
        b_qv,
        w_out,
        res_biases,
        ln_gains,
        ln_shifts,
        w_up,
        b_up,
        w_down,
        short_cotangent,
        long_cotangent,
    ):
        ns, ss, d = short_tokens.shape
        nl, ls, _ = long_tokens.shape
        srows = ns * ss
        heads, hd = b_qv.shape[1], b_qv.shape[2]
        hw = heads * hd
        blk = ls
        kw = dict(nshort=ns, short_slot=ss, heads=heads, blk=blk)
        wires = Wires(n_dp, n_tensor)
        r = w_up.shape[0] // 8

        w1_own = jnp.concatenate([w_qkv.transpose(0, 2, 1).reshape(3 * hw, d), w_out], 0)
        tail = jnp.zeros((d - 2 * hw,), F32)
        small = jnp.stack([b_up[0].astype(F32), jnp.concatenate([b_qv.reshape(2 * hw).astype(F32), tail])])
        small = jnp.concatenate([small, jnp.zeros((6, d), F32)], 0)
        piece = wires.piece(w1_own)
        pr = piece.shape[0]
        piece = jnp.concatenate([small, piece], 0)
        near = [wires.along_tensor(piece, s) for s in (1, n_tensor - 1)]
        far = wires.along_tensor(after(*near), 1)
        row = wires.source * r
        c = row // hw
        place = jnp.stack(
            [row, jnp.where(c < 3, c * 256 + row - c * hw, -1), jnp.where(c < 3, -1, row - 3 * hw)]
        )

        one = np.zeros((256 - hw,), np.float32)
        one[1 : 1 + 3 * heads] = 1.0
        one = jnp.asarray(one)

        def bias_of(sm):
            zero = jnp.zeros((256 - hw,), F32)
            none = jnp.zeros((hw,), F32)
            return jnp.concatenate([sm[1, :hw], zero, none, one, sm[1, hw : 2 * hw], one])[None]

        xs, xl = short_tokens.reshape(srows, d), long_tokens.reshape(-1, d)
        cs, cl = short_cotangent.reshape(srows, d), long_cotangent.reshape(-1, d)
        lens = jnp.concatenate([short_lengths, long_lengths])
        def eighths(*x):
            return wires.whole_eighth(jnp.stack(x)).reshape(len(x), -1, d)

        def join(u, v):
            return jnp.concatenate([u[:1], v, u[1:]], 0)

        t1 = eighths(*[x[8:] for x in near])
        a1, b1 = wires.first_hop(t1)
        bias = after(bias_of(small), *near)
        po = attn_fwd(0, lens, place, xs, xl, w1_own, bias, None, slots=n_tensor, **kw)
        a1, b1, far, *po = lax.optimization_barrier((a1, b1, far, *po))
        z = [near[0], far, near[1]]
        t1b = eighths(far[8:])
        a1b, b1b = wires.first_hop(t1b)
        piece2 = after(jnp.stack([wires.piece(w_up), wires.piece(w_down)]), po[1])
        z2 = [wires.along_tensor(piece2, s) for s in (1, n_tensor - 1)]
        z2.insert(1, wires.along_tensor(z2[0], 1))
        a1, b1b, _ = lax.optimization_barrier((join(a1, a1b), b1b, z2[0]))
        c1 = wires.second_hop(a1)
        w1 = [join(t1, t1b), a1, join(b1, b1b), c1]
        w1 += [wires.to_pair(x) for x in w1[:3]] + [wires.to_pair(after(c1, z2[2]))]
        t2 = eighths(z2[0], z2[2])
        a2, b2 = wires.first_hop(t2)
        for s in range(1, n_tensor):
            po = attn_fwd(s, lens, place, xs, xl, w1, bias_of(z[s - 1]), po, slots=n_tensor, **kw)
            if s == 1:
                a2, b2, mid, *po = lax.optimization_barrier((a2, b2, z2[1], *po))
                t2b = eighths(mid)
                a2b, b2b = wires.first_hop(t2b)
            if s == 2:
                a2b, b2b, *po = lax.optimization_barrier((a2b, b2b, *po))
                t2, a2, b2 = join(t2, t2b), join(a2, a2b), join(b2, b2b)
                c2 = wires.second_hop(a2)
        c2, *po = lax.optimization_barrier((c2, *po))
        w2 = [t2, a2, b2, c2]
        w2 += [wires.to_pair(x) for x in w2]
        p, o = po
        bup = jnp.stack([x[0] for x in [small] + z])
        vecs = jnp.concatenate([res_biases, ln_gains, ln_shifts, jnp.zeros((2, d), BF)], 0).astype(F32)
        es, el, dh, do, gall = ffn_block(
            place, xs, xl, cs, cl, o, vecs, bup, [w1_own, w_up, w_down], w1 + w2, hw, 256
        )
        fl = w_up.shape[1]
        gall = wires.split(gall)
        got = wires.halve_pair(gall)
        dp_own, gw = bwd_own(xs, xl, p, o, do, n_dp=n_dp, **kw)
        gall = wires.sum_pair(gall, after(got, dp_own))
        got = wires.halve_first(gall)
        gw = wires.split(gw)
        gotw = wires.halve_pair(gw)
        nb = (ns * ss + nl * ls) // blk
        rest = (place, p, o, do, dp_own, dh, w1_own, w1, srows)
        gs, gl = bwd_rest(0, nb // 2, None, *rest, **kw)
        got, gotw, gl = lax.optimization_barrier((got, gotw, gl))
        gall = wires.sum_first(gall, got)
        got = wires.halve_second(gall)
        gw = wires.sum_pair(gw, gotw)
        gotw = wires.halve_first(gw)
        (gl,) = bwd_rest(nb // 2, nb, gl, *rest, **kw)
        got, gotw, gl = lax.optimization_barrier((got, gotw, gl))
        gw = wires.sum_first(gw, gotw)
        gotw = wires.halve_second(gw)
        gall = wires.sum_second(gall, got)
        gw = wires.sum_second(gw, gotw)
        small_shard = gall[:, 2 * fl + 256 : 2 * fl + 264].T
        gqkv = gw.reshape(-1, 3, 256)[:, :, :hw].transpose(1, 0, 2)
        kept = hw // n_dp
        qv_shard = jnp.stack([gw[:kept, hw], gw[:kept, hw + 1]]).reshape(2, heads, hd // n_dp)
        return (
            es.reshape(ns, ss, d),
            el.reshape(nl, ls, d),
            gs.reshape(ns, ss, d),
            gl.reshape(nl, ls, d),
            gqkv,
            qv_shard,
            gall[:, 2 * fl : 2 * fl + hw].T,
            small_shard[0:2],
            small_shard[2:4],
            small_shard[4:6],
            gall[:, :fl],
            small_shard[6:7],
            gall[:, fl : 2 * fl].T,
        )

    return on_device


def solution(mesh):
    tok = P("dp", None, None)
    return jax.shard_map(
        make(mesh.shape["dp"], mesh.shape["tensor"]),
        mesh=mesh,
        in_specs=(
            tok,
            P("dp"),
            tok,
            P("dp"),
            P(None, None, "tensor"),
            P(None, "tensor", None),
            P("tensor", None),
            P(),
            P(),
            P(),
            P(None, "tensor"),
            P("tensor", None),
            P("tensor", None),
            tok,
            tok,
        ),
        out_specs=(
            tok,
            tok,
            tok,
            tok,
            P(None, "dp", "tensor"),
            P(None, "tensor", "dp"),
            P("tensor", "dp"),
            P(None, "dp"),
            P(None, "dp"),
            P(None, "dp"),
            P("dp", "tensor"),
            P("tensor", "dp"),
            P("tensor", "dp"),
        ),
        check_vma=False,
    )
```
